128 devices in a mesh: pop: 8 (over y_lo, x), col: 16 (over z, y_hi, core).
Axes of the slice: x: 4, y: 4 (y_hi: 2, y_lo: 2; y = y_hi * 2 + y_lo), z: 4, core: 2. Of those that a mesh axis runs over, the one named last changes fastest.
Arguments:
- acts: bfloat16 [128, 64, 3584], P('pop', None, 'col'), may hold values from -6 to 6
- weight: bfloat16 [3584, 18944], P('pop', 'col'), may hold values from -0.09375 to 0.09375
- input_noise_factor: bfloat16 [128, 4, 3584], P('pop'), may hold values from -1 to 1
- output_noise_factor: bfloat16 [128, 4, 18944], P('pop', None, 'col'), may hold values from -8 to 8
- ranks: int32 [128], P('pop'), may hold values from 0 to 127, each once
Outputs:
- member_out: bfloat16 [128, 64, 18944], P('pop', None, 'col')
- step_dir: float32 [3584, 18944], P('pop', 'col')
- new_weight: bfloat16 [3584, 18944], P('pop', 'col')
The draws below stay inside these ranges and needn't reach their ends.
Inputs may be any that keep to these rules, and one draw needn't show every extreme that they name: `ranks`: every member has a different rank.
All inputs are finite; a program needn't handle non-finite values.
Results may differ from the reference program's by a relative error of at most 0.0034.
Values may be sent and summed in bfloat16 or wider, within the bound.
A program may use at most 192 MiB of HBM per device.

```python
import jax
import jax.numpy as jnp
from jax import lax

D = 3584
F = 18944
RANK = 4
TOK = 64
POPULATION_SIZE = 128


def shared_signs(key):
    coin_flips = jax.random.randint(jax.random.fold_in(key, 7), (POPULATION_SIZE, RANK, 1), 0, 2)
    return (2 * coin_flips - 1).astype(jnp.float32)


def draw_input_noise_factor(key, part):
    sign_table = shared_signs(key)
    shape = (POPULATION_SIZE, RANK, D)
    fresh_part = jnp.clip(jax.random.normal(jax.random.fold_in(key, 1), shape, jnp.float32), -4.0, 4.0)
    amount = 0.6
    common = jnp.clip(jax.random.normal(jax.random.fold_in(key, 11), (D,), jnp.float32), -4.0, 4.0)
    values = (fresh_part + amount * sign_table * common[None, None, :]) * D ** (-0.5)
    return values.astype(jnp.bfloat16)


def draw_output_noise_factor(key, part):
    sign_table = shared_signs(key)
    shape = (POPULATION_SIZE, RANK, F)
    fresh_part = jnp.clip(jax.random.normal(jax.random.fold_in(key, 2), shape, jnp.float32), -4.0, 4.0)
    amount = 0.6
    common = jnp.clip(jax.random.normal(jax.random.fold_in(key, 13), (F,), jnp.float32), -4.0, 4.0)
    values = fresh_part + amount * sign_table * common[None, None, :]
    return values.astype(jnp.bfloat16)


def shard_levels(own_key, shape, split, least, high):
    gain, own = 1.0, jax.random.fold_in(own_key, 6)
    for axis_at, parts in split:
        heights = jnp.exp(jax.random.uniform(jax.random.fold_in(own, axis_at), (parts,), jnp.float32, least / len(split), high / len(split)))
        gain = gain * jnp.repeat(heights, shape[axis_at] // parts).reshape([-1 if axis == axis_at else 1 for axis in range(len(shape))])
    return gain


def bell_draw(key, shape, deviation, bound, split=(), dtype=jnp.bfloat16):
    drawn = jax.random.normal(key, shape, jnp.float32) * deviation
    if len(split) > 0:
        drawn = shard_levels(key, shape, split, -0.22, 0.18) * drawn
    return jnp.clip(drawn, min=-bound, max=bound).astype(dtype)


def setup_inputs(seed: int = 0) -> dict:
    streams_of = jax.random.split(jax.random.key(seed), 6)
    return {
        "acts": bell_draw(streams_of[0], (POPULATION_SIZE, TOK, D), 1.0, 6.0, ((0, 8), (2, 16))),
        "weight": bell_draw(streams_of[1], (D, F), D ** -0.5, 0.09375, ((0, 8), (1, 16))),
        "input_noise_factor": draw_input_noise_factor(jax.random.fold_in(streams_of[5], 71), 0),
        "output_noise_factor": draw_output_noise_factor(jax.random.fold_in(streams_of[5], 71), 0),
        "ranks": jax.random.permutation(streams_of[4], POPULATION_SIZE).astype(jnp.int32),
    }


def reference(acts, weight, input_noise_factor, output_noise_factor, ranks):

    def member_index(items):
        tokens, left, right = items
        base = jnp.dot(tokens, weight, preferred_element_type=jnp.float32)
        lower_bound = jnp.dot(tokens, left.T, preferred_element_type=jnp.float32)
        pert = jnp.dot(lower_bound, right.astype(jnp.float32), precision=lax.Precision.HIGHEST)
        return (base + 0.5 * pert).astype(jnp.bfloat16)
    member_out = lax.map(member_index, (acts, input_noise_factor, output_noise_factor))
    fit = ranks.astype(jnp.float32) / (POPULATION_SIZE - 1) - 0.5
    scaled_update = (output_noise_factor.astype(jnp.float32) * fit[:, None, None]).astype(jnp.bfloat16)
    weight_change = jnp.einsum('vjs,vjg->sg', input_noise_factor.astype(jnp.float32), scaled_update.astype(jnp.float32), precision=lax.Precision.HIGHEST)
    mean_sq = jnp.sum(weight_change * weight_change) / (D * F)
    step_dir = weight_change * lax.rsqrt(mean_sq + 1e-06)
    new_weight = (weight.astype(jnp.float32) + 0.01 * step_dir).astype(jnp.bfloat16)
    return (member_out, step_dir, new_weight)
```

```python
import functools

import jax
import jax.numpy as jnp
from jax import lax
from jax.experimental import pallas as pl
from jax.experimental.pallas import tpu as pltpu
from jax.sharding import PartitionSpec as P

D = 3584
F = 18944
NX = 4
NZ = 4
POP = 8
COL = 16
ROWS = 448
WIDE = 1184
FEAT = 224
TOKENS = 1024
PART = 64
CHUNK = 112
TILE = 256
MESH = pl.DeviceIdType.MESH
BF16 = jnp.bfloat16
F32 = jnp.float32


def kernel(
    acts,
    weight,
    noise,
    scaled,
    out_noise,
    out,
    delta_out,
    total_out,
    wbuf,
    xbuf,
    abuf,
    bbuf,
    acc,
    low,
    delta,
    obuf,
    part,
    parts,
    wsem,
    bsem,
    asem,
    xsem,
    rsem,
    ssem,
    lsem,
):
    pop, col = lax.axis_index("pop"), lax.axis_index("col")
    x, ylo = pop % NX, pop // NX
    z, yhi, core = col // 4, (col // 2) % 2, col % 2

    def pop_at(dy, dx):
        return (ylo * (1 - 2 * dy) + dy) * NX + (x + dx) % NX

    def col_at(dz, dy, dc):
        return (
            ((z + dz) % NZ) * 4
            + (yhi * (1 - 2 * dy) + dy) * 2
            + (core * (1 - 2 * dc) + dc)
        )

    right, left = (pop_at(0, 1), col), (pop_at(0, 3), col)
    pair = (pop_at(1, 0), col)
    up, down = (pop, col_at(1, 0, 0)), (pop, col_at(3, 0, 0))
    far, twin = (pop, col_at(0, 1, 0)), (pop, col_at(0, 0, 1))
    opposite = (pop, col_at(2, 0, 0))
    pop_peers = [
        (dy, dx, (pop_at(dy, dx), col))
        for dy in range(2)
        for dx in range(NX)
        if dy + dx > 0
    ]

    sent = []

    def send(src, dst, sem, device):
        copy = pltpu.make_async_remote_copy(
            src_ref=src,
            dst_ref=dst,
            send_sem=ssem.at[len(sent)],
            recv_sem=sem,
            device_id=device,
            device_id_type=MESH,
        )
        copy.start()
        sent.append(copy)

    def arrive(dst, sem):
        pltpu.make_async_remote_copy(
            src_ref=dst,
            dst_ref=dst,
            send_sem=ssem.at[0],
            recv_sem=sem,
            device_id=right,
            device_id_type=MESH,
        ).wait_recv()

    own = [
        pltpu.make_async_copy(weight, wbuf.at[0], lsem.at[0]),
        pltpu.make_async_copy(acts, xbuf.at[col], lsem.at[1]),
        pltpu.make_async_copy(
            noise.at[pl.ds(2 * pop, 2)], abuf.at[:, pl.ds(0, PART), :], lsem.at[2]
        ),
        pltpu.make_async_copy(scaled, bbuf.at[pl.ds(0, PART), :], lsem.at[3]),
    ]
    for copy in own:
        copy.start()

    barrier = pltpu.get_barrier_semaphore()
    peers = [device for _, _, device in pop_peers] + [up, down, opposite, far, twin]
    for device in peers:
        pl.semaphore_signal(barrier, inc=1, device_id=device, device_id_type=MESH)
    pl.semaphore_wait(barrier, len(peers))

    def w_at(slot, k):
        return wbuf.at[slot, pl.ds(k * CHUNK, CHUNK), :]

    def b_at(slot, k):
        return bbuf.at[pl.ds(slot * PART + k * 32, 32), :]

    def w_send(src_slot, k, dst_slot, device):
        src = weight.at[pl.ds(k * CHUNK, CHUNK), :] if src_slot == 0 else w_at(src_slot, k)
        send(src, w_at(dst_slot, k), wsem.at[dst_slot * 4 + k], device)

    def b_send(src_slot, k, dst_slot, device):
        src = scaled.at[pl.ds(k * 32, 32), :] if src_slot == 0 else b_at(src_slot, k)
        send(src, b_at(dst_slot, k), bsem.at[dst_slot * 2 + k], device)

    def w_arrive(slot, k):
        arrive(w_at(slot, k), wsem.at[slot * 4 + k])

    def b_arrive(slot, k):
        arrive(b_at(slot, k), bsem.at[slot * 2 + k])

    def x_at(c, half=None):
        if half is None:
            return xbuf.at[c]
        return xbuf.at[c, pl.ds(half * (TOKENS // 2), TOKENS // 2), :]

    def x_send(c, half, sem, device, src=None):
        send(x_at(c, half) if src is None else src, x_at(c, half), xsem.at[sem], device)

    for k, device, slot in ((0, right, 3), (1, left, 1), (0, pair, 4), (1, right, 3), (0, left, 1), (1, pair, 4)):
        b_send(0, k, slot, device)
    x_send(col, None, 0, up, acts)
    x_send(col, None, 1, down, acts)
    x_send(col, None, 2, far, acts)
    x_send(col, None, 9, twin, acts)
    for dy, dx, device in pop_peers:
        slot = dy * NX + (NX - dx) % NX
        send(
            noise.at[pl.ds(2 * device[0], 2)],
            abuf.at[:, pl.ds(slot * PART, PART), :],
            asem.at[slot],
            device,
        )
    for k in range(2):
        w_send(0, k, 3, right)
        w_send(0, 3 - k, 1, left)
        w_send(0, k, 4, pair)

    b_arrive(3, 0)
    b_send(3, 0, 2, right)
    b_arrive(1, 1)
    b_send(1, 1, 2, left)
    for k in range(2):
        b_arrive(4, k)
        b_send(4, k, 7, right)
        b_send(4, k, 5, left)
    for k in range(2):
        w_send(0, 2 + k, 3, right)
        w_send(0, 1 - k, 1, left)
        w_send(0, 2 + k, 4, pair)

    c_down, c_up = col_at(3, 0, 0), col_at(1, 0, 0)
    c_far, c_opp = col_at(0, 1, 0), col_at(2, 0, 0)
    f_down, f_up, f_opp = col_at(3, 1, 0), col_at(1, 1, 0), col_at(2, 1, 0)

    def add_low(c):
        low[...] += lax.dot_general(
            xbuf[c],
            noise[c],
            (((1,), (1,)), ((), ())),
            preferred_element_type=F32,
        )

    def x_arrive(c, half, sem):
        arrive(x_at(c, half), xsem.at[sem])

    x_arrive(c_down, None, 0)
    x_send(c_down, 0, 5, up)
    x_send(c_down, None, 10, twin)
    x_arrive(c_up, None, 1)
    x_send(c_up, 1, 6, down)
    x_send(c_up, None, 11, twin)
    x_arrive(c_far, None, 2)
    x_send(c_far, None, 3, up)
    x_send(c_far, None, 4, down)
    x_send(c_far, None, 12, twin)
    for k in range(2):
        b_arrive(2, k)
        b_send(2, k, 6, pair)

    for copy in own:
        copy.wait()
    low[...] = jnp.zeros_like(low)
    for c in (col, c_down, c_up, c_far):
        add_low(c)

    w_arrive(3, 0)
    w_send(3, 0, 2, right)
    w_arrive(1, 3)
    w_send(1, 3, 2, left)
    w_arrive(3, 1)
    w_send(3, 1, 2, right)
    w_arrive(1, 2)
    w_send(1, 2, 2, left)

    b_arrive(3, 1)
    b_arrive(1, 0)
    for slot in (7, 5, 6):
        for k in range(2):
            b_arrive(slot, k)
    for slot in range(1, POP):
        arrive(abuf.at[:, pl.ds(slot * PART, PART), :], asem.at[slot])
    squares = jnp.zeros((), F32)
    for h in range(2):
        block = lax.dot_general(
            abuf[h], bbuf[...], (((0,), (0,)), ((), ())), preferred_element_type=F32
        )
        delta[pl.ds(h * FEAT, FEAT), :] = block
        squares += jnp.sum(block * block)
    write_delta = pltpu.make_async_copy(delta, delta_out, lsem.at[4])
    write_delta.start()
    part[0] = jnp.full((8, 128), squares, F32)

    for k in range(4):
        w_arrive(4, k)
    x_arrive(f_down, None, 3)
    x_send(f_down, 0, 7, up)
    x_send(f_down, None, 13, twin)
    x_arrive(f_up, None, 4)
    x_send(f_up, 1, 8, down)
    x_send(f_up, None, 14, twin)

    send(part.at[0], parts.at[0], rsem.at[0], twin)
    arrive(parts.at[0], rsem.at[0])
    part[1] = part[0] + parts[0]
    add_low(f_down)
    add_low(f_up)
    for i, device in enumerate((up, opposite, down)):
        send(part.at[1], parts.at[1 + i], rsem.at[1 + i], device)
    for i in range(3):
        arrive(parts.at[1 + i], rsem.at[1 + i])
    part[2] = part[1] + parts[1] + parts[2] + parts[3]

    x_arrive(c_opp, 0, 5)
    x_send(c_opp, 0, 15, twin)
    x_arrive(c_opp, 1, 6)
    x_send(c_opp, 1, 16, twin)
    add_low(c_opp)
    send(part.at[2], parts.at[4], rsem.at[4], far)
    arrive(parts.at[4], rsem.at[4])
    part[3] = part[2] + parts[4]
    for k in range(2):
        w_send(4, k, 7, right)
        w_send(4, k, 5, left)
    x_arrive(f_opp, 0, 7)
    x_send(f_opp, 0, 17, twin)
    x_arrive(f_opp, 1, 8)
    x_send(f_opp, 1, 18, twin)
    add_low(f_opp)
    for dy, dx, device in pop_peers:
        i = 4 + dy * NX + dx
        send(part.at[3], parts.at[i], rsem.at[i], device)
    for k in range(2, 4):
        w_send(4, k, 7, right)
        w_send(4, k, 5, left)

    for k in (0, 3):
        w_arrive(2, k)
        w_send(2, k, 6, pair)
    for (dz, dy), sems in (
        ((0, 0), ((None, 9),)),
        ((3, 0), ((None, 10),)),
        ((1, 0), ((None, 11),)),
        ((0, 1), ((None, 12),)),
        ((3, 1), ((None, 13),)),
        ((1, 1), ((None, 14),)),
        ((2, 0), ((0, 15), (1, 16))),
        ((2, 1), ((0, 17), (1, 18))),
    ):
        c = col_at(dz, dy, 1)
        for half, sem in sems:
            x_arrive(c, half, sem)
        add_low(c)
    for k in (1, 2):
        w_arrive(2, k)
        w_send(2, k, 6, pair)

    rank = lax.broadcasted_iota(jnp.int32, (TOKENS, PART), 1) // 4
    token = lax.broadcasted_iota(jnp.int32, (TOKENS, PART), 0) // 64
    rest = jnp.where(rank == token, low[...] * 0.5, 0.0)
    low[...] = rest

    def rows(i):
        return pl.ds(pl.multiple_of(i * TILE, TILE), TILE)

    @pl.loop(0, TOKENS // TILE)
    def _(i):
        left_over = low[rows(i), :]
        total = None
        for _ in range(3):
            term = left_over.astype(BF16)
            left_over = left_over - term.astype(F32)
            product = jnp.dot(term, out_noise[...], preferred_element_type=F32)
            total = product if total is None else total + product
        acc[rows(i), :] = total

    def dot(i, slot, h):
        c = 2 * pop_at(slot // NX, slot % NX) + h
        return jnp.dot(
            xbuf[c, rows(i), :],
            wbuf[slot, pl.ds(h * FEAT, FEAT), :],
            preferred_element_type=F32,
        )

    def blocks(slots, halves):
        @pl.loop(0, TOKENS // TILE)
        def _(i):
            for slot in slots:
                for h in halves:
                    acc[rows(i), :] += dot(i, slot, h)

    blocks((0, 4), (0, 1))
    for k in range(2, 4):
        w_arrive(3, k)
    for k in range(2):
        w_arrive(1, k)
    blocks((1, 3), (0, 1))
    blocks((2,), (0, 1))

    total = part[3]
    for dy, dx, device in pop_peers:
        slot = 4 + dy * NX + dx
        arrive(parts.at[slot], rsem.at[slot])
        total = total + parts[slot]
    part[4] = total
    write_total = pltpu.make_async_copy(part.at[4], total_out, lsem.at[5])
    write_total.start()

    for slot in (7, 5):
        for k in range(2):
            w_arrive(slot, k)
    for k in (0, 1):
        w_arrive(6, k)
    blocks((5, 7, 6), (0,))
    for slot in (7, 5):
        for k in range(2, 4):
            w_arrive(slot, k)
    for k in (3, 2):
        w_arrive(6, k)

    for i in range(TOKENS // TILE):
        tile = pl.ds(i * TILE, TILE)
        value = acc[tile, :]
        for slot in (5, 7, 6):
            value = value + dot(i, slot, 1)
        obuf[tile, :] = value.astype(BF16)
        pltpu.make_async_copy(obuf.at[tile, :], out.at[tile, :], lsem.at[6 + i]).start()

    for i in range(TOKENS // TILE):
        tile = pl.ds(i * TILE, TILE)
        pltpu.make_async_copy(obuf.at[tile, :], out.at[tile, :], lsem.at[6 + i]).wait()
    write_delta.wait()
    write_total.wait()
    for copy in sent:
        copy.wait_send()


def body(acts, weight, input_noise_factor, output_noise_factor, ranks):
    fit = ranks.astype(F32) / (16 * POP - 1) - 0.5
    scaled = (output_noise_factor.astype(F32) * fit[:, None, None]).astype(BF16)
    noise = input_noise_factor.reshape(PART, COL, FEAT).transpose(1, 0, 2)
    anywhere = pl.BlockSpec(memory_space=pl.ANY)
    vmem = pl.BlockSpec(memory_space=pltpu.VMEM)
    flat, delta, total = pl.pallas_call(
        kernel,
        out_shape=(
            jax.ShapeDtypeStruct((TOKENS, WIDE), BF16),
            jax.ShapeDtypeStruct((ROWS, WIDE), F32),
            jax.ShapeDtypeStruct((8, 128), F32),
        ),
        in_specs=[anywhere, anywhere, vmem, anywhere, vmem],
        out_specs=(anywhere, anywhere, anywhere),
        scratch_shapes=[
            pltpu.VMEM((POP, ROWS, WIDE), BF16),
            pltpu.VMEM((COL, TOKENS, FEAT), BF16),
            pltpu.VMEM((2, POP * PART, FEAT), BF16),
            pltpu.VMEM((POP * PART, WIDE), BF16),
            pltpu.VMEM((TOKENS, WIDE), F32),
            pltpu.VMEM((TOKENS, PART), F32),
            pltpu.VMEM((ROWS, WIDE), F32),
            pltpu.VMEM((TOKENS, WIDE), BF16),
            pltpu.VMEM((5, 8, 128), F32),
            pltpu.VMEM((12, 8, 128), F32),
            pltpu.SemaphoreType.DMA((POP * 4,)),
            pltpu.SemaphoreType.DMA((POP * 2,)),
            pltpu.SemaphoreType.DMA((POP,)),
            pltpu.SemaphoreType.DMA((19,)),
            pltpu.SemaphoreType.DMA((12,)),
            pltpu.SemaphoreType.DMA((96,)),
            pltpu.SemaphoreType.DMA((10,)),
        ],
        compiler_params=pltpu.CompilerParams(
            collective_id=0, has_side_effects=True, vmem_limit_bytes=62 * 1024 * 1024
        ),
    )(
        acts.reshape(TOKENS, FEAT),
        weight,
        noise,
        scaled.reshape(PART, WIDE),
        output_noise_factor.reshape(PART, WIDE),
    )
    mean_sq = total[0, 0] / (D * F)
    step_dir = delta * lax.rsqrt(mean_sq + 1e-06)
    new_weight = (weight.astype(F32) + 0.01 * step_dir).astype(BF16)
    return (flat.reshape(16, 64, WIDE), step_dir, new_weight)


def solution(mesh):
    in_specs = (
        P("pop", None, "col"),
        P("pop", "col"),
        P("pop", None, None),
        P("pop", None, "col"),
        P("pop"),
    )
    out_specs = (P("pop", None, "col"), P("pop", "col"), P("pop", "col"))
    return jax.shard_map(body, mesh=mesh, in_specs=in_specs, out_specs=out_specs, check_vma=False)
```

```python
import jax
import jax.numpy as jnp
from jax import lax
from jax.experimental import pallas as pl
from jax.experimental.pallas import tpu as pltpu
from jax.sharding import PartitionSpec as P

D = 3584
F = 18944
NX = 4
NZ = 4
POP = 8
COL = 16
MEMBERS = 16
ROWS = 448
WIDE = 1184
MAIN = 1152
REST = WIDE - MAIN
FEAT = 224
TOKENS = 1024
PART = 64
GROUPS = ((0, 256), (256, 256), (512, 256), (768, 256), (1024, 128))
NG = len(GROUPS)
TILE = 256
MESH = pl.DeviceIdType.MESH
BF16 = jnp.bfloat16
F32 = jnp.float32


def kernel(
    acts,
    weight,
    noise_in,
    out_in,
    ranks_in,
    out,
    step_out,
    new_out,
    wbuf,
    xbuf,
    abuf,
    bbuf,
    tbuf,
    ranks,
    noise_raw,
    out_raw,
    noise,
    out_noise,
    acc,
    low,
    delta,
    part,
    parts,
    wsem,
    bsem,
    tsem,
    asem,
    xsem,
    rsem,
    ssem,
    lsem,
):
    pop, col = lax.axis_index("pop"), lax.axis_index("col")
    x, ylo = pop % NX, pop // NX
    z, yhi, core = col // 4, (col // 2) % 2, col % 2
    mine = z * 2 + core

    def pop_at(dy, dx):
        return (ylo * (1 - 2 * dy) + dy) * NX + (x + dx) % NX

    def col_at(dz, dy, dc):
        return (
            ((z + dz) % NZ) * 4
            + (yhi * (1 - 2 * dy) + dy) * 2
            + (core * (1 - 2 * dc) + dc)
        )

    right, left = (pop_at(0, 1), col), (pop_at(0, 3), col)
    pair = (pop_at(1, 0), col)
    up, down = (pop, col_at(1, 0, 0)), (pop, col_at(3, 0, 0))
    far, twin = (pop, col_at(0, 1, 0)), (pop, col_at(0, 0, 1))
    pop_peers = [
        (dy * NX + dx, (pop_at(dy, dx), col))
        for dy in range(2)
        for dx in range(NX)
        if dy + dx > 0
    ]
    col_peers = [
        (dz * 2 + dc, (pop, col_at(dz, 0, dc)))
        for dz in range(NZ)
        for dc in range(2)
        if dz + dc > 0
    ]

    sent = []

    def send(src, dst, sem, device):
        copy = pltpu.make_async_remote_copy(
            src_ref=src,
            dst_ref=dst,
            send_sem=ssem.at[len(sent)],
            recv_sem=sem,
            device_id=device,
            device_id_type=MESH,
        )
        copy.start()
        sent.append(copy)

    def arrive(dst, sem):
        pltpu.make_async_remote_copy(
            src_ref=dst,
            dst_ref=dst,
            send_sem=ssem.at[0],
            recv_sem=sem,
            device_id=right,
            device_id_type=MESH,
        ).wait_recv()

    own_noise = pltpu.make_async_copy(noise_in, noise_raw, lsem.at[0])
    own_out = pltpu.make_async_copy(out_in, out_raw, lsem.at[1])
    own_weight = pltpu.make_async_copy(weight, wbuf.at[0], lsem.at[2])
    own_acts = pltpu.make_async_copy(acts, xbuf.at[col], lsem.at[3])
    own_ranks = pltpu.make_async_copy(ranks_in, ranks, lsem.at[6])
    for copy in (own_ranks, own_out, own_noise, own_weight, own_acts):
        copy.start()

    barrier = pltpu.get_barrier_semaphore()
    peers = [device for _, device in pop_peers + col_peers] + [far]
    for device in peers:
        pl.semaphore_signal(barrier, inc=1, device_id=device, device_id_type=MESH)
    pl.semaphore_wait(barrier, len(peers))

    def piece(h, j):
        return pl.ds(h * FEAT, FEAT), pl.ds(*GROUPS[j])

    def w_at(slot, h, j):
        r, c = piece(h, j)
        return wbuf.at[slot, r, c]

    def w_send(src_slot, h, j, dst_slot, device):
        r, c = piece(h, j)
        src = weight.at[r, c] if src_slot == 0 else wbuf.at[src_slot, r, c]
        send(src, w_at(dst_slot, h, j), wsem.at[(dst_slot * 2 + h) * NG + j], device)

    def w_arrive(slot, h, j):
        arrive(w_at(slot, h, j), wsem.at[(slot * 2 + h) * NG + j])

    def b_at(slot, k):
        return bbuf.at[pl.ds(slot * PART + k * 32, 32), pl.ds(0, MAIN)]

    def t_at(slot, k):
        return tbuf.at[slot, pl.ds(k * 64, 64), :]

    def b_send(src_slot, k, dst_slot, device):
        send(b_at(src_slot, k), b_at(dst_slot, k), bsem.at[dst_slot * 2 + k], device)
        send(t_at(src_slot, k), t_at(dst_slot, k), tsem.at[dst_slot * 2 + k], device)

    def b_arrive(slot, k):
        arrive(b_at(slot, k), bsem.at[slot * 2 + k])
        arrive(t_at(slot, k), tsem.at[slot * 2 + k])

    def x_at(c, half=None):
        if half is None:
            return xbuf.at[c]
        return xbuf.at[c, pl.ds(half * (TOKENS // 2), TOKENS // 2), :]

    def x_send(c, half, sem, device, src=None):
        send(x_at(c, half) if src is None else src, x_at(c, half), xsem.at[sem], device)

    def x_arrive(c, half, sem):
        arrive(x_at(c, half), xsem.at[sem])

    to_right = [(h, j) for h in (0, 1) for j in range(NG)]
    to_left = [(h, j) for h in (1, 0) for j in range(NG)]
    to_pair = [(h, j) for j in range(NG) for h in (0, 1)]

    def own_pieces(first, last):
        for i in range(first, last):
            w_send(0, *to_right[i], 3, right)
            w_send(0, *to_left[i], 1, left)

    def own_to_pair(first, last):
        for i in range(first, last):
            w_send(0, *to_pair[i], 4, pair)

    x_send(col, None, 0, up, acts)
    x_send(col, None, 1, down, acts)
    own_pieces(0, 2)
    own_to_pair(0, 2)
    x_send(col, None, 2, far, acts)
    x_send(col, None, 9, twin, acts)

    own_ranks.wait()
    own_out.wait()
    raw = jnp.concatenate([out_raw[m].astype(F32) for m in range(MEMBERS)], axis=0)
    out_noise[...] = raw.astype(BF16)
    fit = jnp.concatenate(
        [
            jnp.full((4, 1), ranks[m].astype(F32), F32) / (MEMBERS * POP - 1) - 0.5
            for m in range(MEMBERS)
        ],
        axis=0,
    )
    scaled = raw * fit
    bbuf[pl.ds(0, PART), :] = scaled.astype(BF16)
    own_weight.wait()
    last = wbuf[0, :, pl.ds(MAIN, REST)].astype(F32)
    tbuf[0, pl.ds(0, 112), :] = jnp.concatenate(
        [last[g * 112 : g * 112 + 112] for g in range(4)], axis=1
    ).astype(BF16)
    tbuf[0, pl.ds(112, 16), :] = jnp.concatenate(
        [scaled[g * 16 : g * 16 + 16, MAIN:WIDE] for g in range(4)], axis=1
    ).astype(BF16)
    own_noise.wait()
    wide = jnp.concatenate([noise_raw[m].astype(F32) for m in range(MEMBERS)], axis=0)
    for c in range(COL):
        noise[c] = wide[:, c * FEAT : (c + 1) * FEAT].astype(BF16)

    for k, device, slot in ((0, right, 3), (1, left, 1), (0, pair, 4), (1, right, 3), (0, left, 1), (1, pair, 4)):
        b_send(0, k, slot, device)

    def a_at(slot):
        return abuf.at[:, pl.ds(slot * PART, PART), :]

    target = (ylo + mine // NX) % 2 * NX + (x + NX - mine % NX) % NX
    fetch = pltpu.make_async_remote_copy(
        src_ref=noise.at[pl.ds(2 * target, 2)],
        dst_ref=a_at(mine),
        send_sem=lsem.at[4],
        recv_sem=asem.at[0],
        device_id=(target, col),
        device_id_type=MESH,
    )
    keep = pltpu.make_async_copy(noise.at[pl.ds(2 * pop, 2)], a_at(0), lsem.at[5])

    @pl.when(mine > 0)
    def _():
        fetch.start()

    @pl.when(mine == 0)
    def _():
        keep.start()

    own_pieces(2, 6)
    own_to_pair(2, 7)

    c_down, c_up = col_at(3, 0, 0), col_at(1, 0, 0)
    c_far, c_opp = col_at(0, 1, 0), col_at(2, 0, 0)
    f_down, f_up, f_opp = col_at(3, 1, 0), col_at(1, 1, 0), col_at(2, 1, 0)

    def add_low(c):
        low[...] += lax.dot_general(
            xbuf[c],
            noise[c],
            (((1,), (1,)), ((), ())),
            preferred_element_type=F32,
        )

    low[...] = jnp.zeros_like(low)
    own_acts.wait()
    add_low(col)

    x_arrive(c_down, None, 0)
    x_send(c_down, 0, 5, up)
    x_send(c_down, None, 10, twin)
    x_arrive(c_up, None, 1)
    x_send(c_up, 1, 6, down)
    x_send(c_up, None, 11, twin)

    b_arrive(3, 0)
    b_send(3, 0, 2, right)
    b_arrive(1, 1)
    b_send(1, 1, 2, left)
    for k in range(2):
        b_arrive(4, k)
        b_send(4, k, 7, right)
        b_send(4, k, 5, left)
    own_pieces(6, 10)

    @pl.when(mine > 0)
    def _():
        fetch.wait()

    @pl.when(mine == 0)
    def _():
        keep.wait()

    for i, device in col_peers:
        send(a_at(mine), a_at(mine), asem.at[i], device)

    add_low(c_down)
    add_low(c_up)
    x_arrive(c_far, None, 2)
    x_send(c_far, None, 3, up)
    x_send(c_far, None, 4, down)
    x_send(c_far, None, 12, twin)
    for k in range(2):
        b_arrive(2, k)
        b_send(2, k, 6, pair)
    own_to_pair(7, 10)
    add_low(c_far)

    for j in range(NG):
        w_arrive(3, 0, j)
        w_send(3, 0, j, 2, right)
        w_arrive(1, 1, j)
        w_send(1, 1, j, 2, left)

    b_arrive(3, 1)
    b_arrive(1, 0)
    for slot in (7, 5, 6):
        for k in range(2):
            b_arrive(slot, k)
    for i, _ in col_peers:
        dz, dc = i // 2, i % 2
        sender = ((z + NZ - dz) % NZ) * 2 + (core * (1 - 2 * dc) + dc)
        arrive(a_at(sender), asem.at[i])

    @pl.loop(1, POP)
    def _(slot):
        packed = tbuf[slot].astype(F32)
        for g in range(4):
            mid = packed[:, g * REST : (g + 1) * REST].astype(BF16)
            wbuf[slot, pl.ds(g * 112, 112), pl.ds(MAIN, REST)] = mid[:112]
            bbuf[
                pl.ds(pl.multiple_of(slot * PART + g * 16, 16), 16), pl.ds(MAIN, REST)
            ] = mid[112:]

    squares = jnp.zeros((), F32)
    for h in range(2):
        block = lax.dot_general(
            abuf[h], bbuf[...], (((0,), (0,)), ((), ())), preferred_element_type=F32
        )
        delta[pl.ds(h * FEAT, FEAT), :] = block
        squares += jnp.sum(block * block)
    part[0] = jnp.full((8, 128), squares, F32)

    x_arrive(f_down, None, 3)
    x_send(f_down, 0, 7, up)
    x_send(f_down, None, 13, twin)
    x_arrive(f_up, None, 4)
    x_send(f_up, 1, 8, down)
    x_send(f_up, None, 14, twin)

    for i, device in col_peers:
        send(part.at[0], parts.at[i], rsem.at[i], device)
    add_low(f_down)
    add_low(f_up)

    for j in range(2):
        w_arrive(2, 0, j)
        w_send(2, 0, j, 6, pair)
        w_arrive(2, 1, j)
        w_send(2, 1, j, 6, pair)

    for i, _ in col_peers:
        arrive(parts.at[i], rsem.at[i])
    total = part[0]
    for i, _ in col_peers:
        total = total + parts[i]
    part[1] = total

    x_arrive(c_opp, 0, 5)
    x_send(c_opp, 0, 15, twin)
    x_arrive(c_opp, 1, 6)
    x_send(c_opp, 1, 16, twin)
    send(part.at[1], parts.at[8], rsem.at[8], far)
    add_low(c_opp)
    x_arrive(f_opp, 0, 7)
    x_send(f_opp, 0, 17, twin)
    x_arrive(f_opp, 1, 8)
    x_send(f_opp, 1, 18, twin)
    add_low(f_opp)

    def pass_on(first, last):
        for i in range(first, last):
            h, j = to_pair[i]
            w_arrive(4, h, j)
            w_send(4, h, j, 7, right)
            w_send(4, h, j, 5, left)

    pass_on(0, 2)
    for (dz, dy), sems in (
        ((0, 0), ((None, 9),)),
        ((3, 0), ((None, 10),)),
        ((1, 0), ((None, 11),)),
        ((0, 1), ((None, 12),)),
        ((3, 1), ((None, 13),)),
        ((1, 1), ((None, 14),)),
        ((2, 0), ((0, 15), (1, 16))),
        ((2, 1), ((0, 17), (1, 18))),
    ):
        c = col_at(dz, dy, 1)
        for half, sem in sems:
            x_arrive(c, half, sem)
        add_low(c)
    for j in range(2, NG):
        w_arrive(2, 0, j)
        w_send(2, 0, j, 6, pair)
        w_arrive(2, 1, j)
        w_send(2, 1, j, 6, pair)

    arrive(parts.at[8], rsem.at[8])
    part[2] = part[1] + parts[8]
    pass_on(2, 3)

    rank = lax.broadcasted_iota(jnp.int32, (TOKENS, PART), 1) // 4
    token = lax.broadcasted_iota(jnp.int32, (TOKENS, PART), 0) // 64
    low[...] = jnp.where(rank == token, low[...] * 0.5, 0.0)

    def rows(i):
        return pl.ds(pl.multiple_of(i * TILE, TILE), TILE)

    @pl.loop(0, TOKENS // TILE)
    def _(i):
        left_over = low[rows(i), :]
        value = None
        for _ in range(3):
            term = left_over.astype(BF16)
            left_over = left_over - term.astype(F32)
            product = jnp.dot(term, out_noise[...], preferred_element_type=F32)
            value = product if value is None else value + product
        acc[rows(i), :] = value

    for i, device in pop_peers:
        send(part.at[2], parts.at[8 + i], rsem.at[8 + i], device)
    pass_on(3, 5)

    def dot(i, slot, h, cols):
        c = 2 * pop_at(slot // NX, slot % NX) + h
        return jnp.dot(
            xbuf[c, rows(i), :],
            wbuf[slot, pl.ds(h * FEAT, FEAT), cols],
            preferred_element_type=F32,
        )

    everything = pl.ds(0, WIDE)

    def blocks(slot):
        @pl.loop(0, TOKENS // TILE)
        def _(i):
            for h in range(2):
                acc[rows(i), :] += dot(i, slot, h, everything)

    blocks(0)
    pass_on(5, 7)
    for j in range(NG):
        w_arrive(3, 1, j)
        w_arrive(1, 0, j)
    blocks(1)
    pass_on(7, 9)
    blocks(3)
    pass_on(9, 10)
    blocks(4)
    blocks(2)

    total = part[2]
    for i, _ in pop_peers:
        arrive(parts.at[8 + i], rsem.at[8 + i])
        total = total + parts[8 + i]
    scale = lax.rsqrt(total / (D * F) + 1e-06)[0:1, 0:1]
    step = delta[...] * scale
    step_out[...] = step
    new_out[...] = (wbuf[0].astype(F32) + 0.01 * step).astype(BF16)
    for j in range(NG):
        for h in range(2):
            for slot in (5, 7, 6):
                w_arrive(slot, h, j)
        first, n = GROUPS[j]
        cols = pl.ds(first, n if j < NG - 1 else WIDE - first)

        @pl.loop(0, TOKENS // TILE)
        def _(i):
            value = acc[rows(i), cols]
            for slot in (5, 7, 6):
                for h in range(2):
                    value = value + dot(i, slot, h, cols)
            out[rows(i), cols] = value.astype(BF16)


    for copy in sent:
        copy.wait_send()


def put_out(out_v, step_v, new_v, out, step_out, new_out, sem):
    writes = [
        pltpu.make_async_copy(src, dst, sem.at[i])
        for i, (src, dst) in enumerate(
            ((step_v, step_out), (out_v, out), (new_v, new_out))
        )
    ]
    for copy in writes:
        copy.start()
    for copy in writes:
        copy.wait()


def body(acts, weight, input_noise_factor, output_noise_factor, ranks):
    hbm = pl.BlockSpec(memory_space=pltpu.HBM)
    vmem = pl.BlockSpec(memory_space=pltpu.VMEM)
    made = pl.pallas_call(
        kernel,
        out_shape=(
            pltpu.VMEM((TOKENS, WIDE), BF16),
            pltpu.VMEM((ROWS, WIDE), F32),
            pltpu.VMEM((ROWS, WIDE), BF16),
        ),
        in_specs=[hbm] * 5,
        out_specs=(vmem,) * 3,
        scratch_shapes=[
            pltpu.VMEM((POP, ROWS, WIDE), BF16),
            pltpu.VMEM((COL, TOKENS, FEAT), BF16),
            pltpu.VMEM((2, POP * PART, FEAT), BF16),
            pltpu.VMEM((POP * PART, WIDE), BF16),
            pltpu.VMEM((POP, 128, 128), BF16),
            pltpu.SMEM((MEMBERS,), jnp.int32),
            pltpu.VMEM((MEMBERS, 4, D), BF16),
            pltpu.VMEM((MEMBERS, 4, WIDE), BF16),
            pltpu.VMEM((COL, PART, FEAT), BF16),
            pltpu.VMEM((PART, WIDE), BF16),
            pltpu.VMEM((TOKENS, WIDE), F32),
            pltpu.VMEM((TOKENS, PART), F32),
            pltpu.VMEM((ROWS, WIDE), F32),
            pltpu.VMEM((3, 8, 128), F32),
            pltpu.VMEM((16, 8, 128), F32),
            pltpu.SemaphoreType.DMA((POP * 2 * NG,)),
            pltpu.SemaphoreType.DMA((POP * 2,)),
            pltpu.SemaphoreType.DMA((POP * 2,)),
            pltpu.SemaphoreType.DMA((8,)),
            pltpu.SemaphoreType.DMA((19,)),
            pltpu.SemaphoreType.DMA((16,)),
            pltpu.SemaphoreType.DMA((192,)),
            pltpu.SemaphoreType.DMA((13,)),
        ],
        compiler_params=pltpu.CompilerParams(
            collective_id=0, has_side_effects=True, vmem_limit_bytes=57 * 1024 * 1024
        ),
    )(
        acts.reshape(TOKENS, FEAT),
        weight,
        input_noise_factor,
        output_noise_factor,
        pltpu.with_memory_space_constraint(ranks, pltpu.HBM),
    )
    out, step_dir, new_weight = pl.pallas_call(
        put_out,
        out_shape=(
            jax.ShapeDtypeStruct((TOKENS, WIDE), BF16),
            jax.ShapeDtypeStruct((ROWS, WIDE), F32),
            jax.ShapeDtypeStruct((ROWS, WIDE), BF16),
        ),
        in_specs=[vmem] * 3,
        out_specs=(hbm,) * 3,
        scratch_shapes=[pltpu.SemaphoreType.DMA((3,))],
        compiler_params=pltpu.CompilerParams(vmem_limit_bytes=16 * 1024 * 1024),
    )(*made)
    return (out.reshape(MEMBERS, TOKENS // MEMBERS, WIDE), step_dir, new_weight)


def solution(mesh):
    in_specs = (
        P("pop", None, "col"),
        P("pop", "col"),
        P("pop", None, None),
        P("pop", None, "col"),
        P("pop"),
    )
    out_specs = (P("pop", None, "col"), P("pop", "col"), P("pop", "col"))
    return jax.shard_map(body, mesh=mesh, in_specs=in_specs, out_specs=out_specs, check_vma=False)
```

```python
import jax
import jax.numpy as jnp
from jax import lax
from jax.experimental import pallas as pl
from jax.experimental.pallas import tpu as pltpu
from jax.sharding import PartitionSpec as P

D = 3584
F = 18944
NX = 4
NZ = 4
POP = 8
COL = 16
MEMBERS = 16
ROWS = 448
WIDE = 1184
MAIN = 1152
REST = WIDE - MAIN
FEAT = 224
TOKENS = 1024
PART = 64
GROUPS = ((0, 256), (256, 256), (512, 256), (768, 256), (1024, 128))
NG = len(GROUPS)
TILE = 256
MESH = pl.DeviceIdType.MESH
BF16 = jnp.bfloat16
F32 = jnp.float32


def kernel(
    acts,
    weight,
    noise_in,
    out_in,
    ranks_in,
    out,
    step_out,
    new_out,
    wbuf,
    xbuf,
    abuf,
    bbuf,
    tbuf,
    ranks,
    noise_raw,
    out_raw,
    noise,
    out_noise,
    acc,
    low,
    delta,
    part,
    parts,
    wsem,
    bsem,
    tsem,
    asem,
    xsem,
    rsem,
    ssem,
    lsem,
):
    pop, col = lax.axis_index("pop"), lax.axis_index("col")
    x, ylo = pop % NX, pop // NX
    z, yhi, core = col // 4, (col // 2) % 2, col % 2
    mine = z * 2 + core

    def pop_at(dy, dx):
        return (ylo * (1 - 2 * dy) + dy) * NX + (x + dx) % NX

    def col_at(dz, dy, dc):
        return (
            ((z + dz) % NZ) * 4
            + (yhi * (1 - 2 * dy) + dy) * 2
            + (core * (1 - 2 * dc) + dc)
        )

    right, left = (pop_at(0, 1), col), (pop_at(0, 3), col)
    pair = (pop_at(1, 0), col)
    up, down = (pop, col_at(1, 0, 0)), (pop, col_at(3, 0, 0))
    far, twin = (pop, col_at(0, 1, 0)), (pop, col_at(0, 0, 1))
    pop_peers = [
        (dy * NX + dx, (pop_at(dy, dx), col))
        for dy in range(2)
        for dx in range(NX)
        if dy + dx > 0
    ]
    col_peers = [
        (dz * 2 + dc, (pop, col_at(dz, 0, dc)))
        for dz in range(NZ)
        for dc in range(2)
        if dz + dc > 0
    ]

    sent = []

    def send(src, dst, sem, device):
        copy = pltpu.make_async_remote_copy(
            src_ref=src,
            dst_ref=dst,
            send_sem=ssem.at[len(sent)],
            recv_sem=sem,
            device_id=device,
            device_id_type=MESH,
        )
        copy.start()
        sent.append(copy)

    def arrive(dst, sem):
        pltpu.make_async_remote_copy(
            src_ref=dst,
            dst_ref=dst,
            send_sem=ssem.at[0],
            recv_sem=sem,
            device_id=right,
            device_id_type=MESH,
        ).wait_recv()

    own_noise = pltpu.make_async_copy(noise_in, noise_raw, lsem.at[0])
    own_out = pltpu.make_async_copy(out_in, out_raw, lsem.at[1])
    own_weight = pltpu.make_async_copy(weight, wbuf.at[0], lsem.at[2])
    own_acts = pltpu.make_async_copy(acts, xbuf.at[col], lsem.at[3])
    own_ranks = pltpu.make_async_copy(ranks_in, ranks, lsem.at[6])
    for copy in (own_ranks, own_out, own_noise, own_weight, own_acts):
        copy.start()

    barrier = pltpu.get_barrier_semaphore()
    peers = [device for _, device in pop_peers + col_peers] + [far]
    for device in peers:
        pl.semaphore_signal(barrier, inc=1, device_id=device, device_id_type=MESH)
    pl.semaphore_wait(barrier, len(peers))

    def piece(h, j):
        return pl.ds(h * FEAT, FEAT), pl.ds(*GROUPS[j])

    def w_at(slot, h, j):
        r, c = piece(h, j)
        return wbuf.at[slot, r, c]

    def w_send(src_slot, h, j, dst_slot, device):
        r, c = piece(h, j)
        src = weight.at[r, c] if src_slot == 0 else wbuf.at[src_slot, r, c]
        send(src, w_at(dst_slot, h, j), wsem.at[(dst_slot * 2 + h) * NG + j], device)

    def w_arrive(slot, h, j):
        arrive(w_at(slot, h, j), wsem.at[(slot * 2 + h) * NG + j])

    def b_at(slot, k):
        return bbuf.at[pl.ds(slot * PART + k * 32, 32), pl.ds(0, MAIN)]

    def t_at(slot, k):
        return tbuf.at[slot, pl.ds(k * 64, 64), :]

    def b_send(src_slot, k, dst_slot, device):
        send(b_at(src_slot, k), b_at(dst_slot, k), bsem.at[dst_slot * 2 + k], device)
        send(t_at(src_slot, k), t_at(dst_slot, k), tsem.at[dst_slot * 2 + k], device)

    def b_arrive(slot, k):
        arrive(b_at(slot, k), bsem.at[slot * 2 + k])
        arrive(t_at(slot, k), tsem.at[slot * 2 + k])

    def x_at(c, half=None):
        if half is None:
            return xbuf.at[c]
        return xbuf.at[c, pl.ds(half * (TOKENS // 2), TOKENS // 2), :]

    def x_send(c, half, sem, device, src=None):
        send(x_at(c, half) if src is None else src, x_at(c, half), xsem.at[sem], device)

    def x_arrive(c, half, sem):
        arrive(x_at(c, half), xsem.at[sem])

    to_right = [(h, j) for h in (0, 1) for j in range(NG)]
    to_left = [(h, j) for h in (1, 0) for j in range(NG)]
    to_pair = [(h, j) for j in range(NG) for h in (0, 1)]

    def own_pieces(first, last):
        for i in range(first, last):
            w_send(0, *to_right[i], 3, right)
            w_send(0, *to_left[i], 1, left)

    def own_to_pair(first, last):
        for i in range(first, last):
            w_send(0, *to_pair[i], 4, pair)

    x_send(col, None, 0, up, acts)
    x_send(col, None, 1, down, acts)
    own_pieces(0, 2)
    own_to_pair(0, 1)
    x_send(col, None, 9, twin, acts)

    own_ranks.wait()
    own_out.wait()
    raw = jnp.concatenate([out_raw[m].astype(F32) for m in range(MEMBERS)], axis=0)
    out_noise[...] = raw.astype(BF16)
    fit = jnp.concatenate(
        [
            jnp.full((4, 1), ranks[m].astype(F32), F32) / (MEMBERS * POP - 1) - 0.5
            for m in range(MEMBERS)
        ],
        axis=0,
    )
    scaled = raw * fit
    bbuf[pl.ds(0, PART), :] = scaled.astype(BF16)
    own_weight.wait()
    last = wbuf[0, :, pl.ds(MAIN, REST)].astype(F32)
    tbuf[0, pl.ds(0, 112), :] = jnp.concatenate(
        [last[g * 112 : g * 112 + 112] for g in range(4)], axis=1
    ).astype(BF16)
    tbuf[0, pl.ds(112, 16), :] = jnp.concatenate(
        [scaled[g * 16 : g * 16 + 16, MAIN:WIDE] for g in range(4)], axis=1
    ).astype(BF16)
    own_noise.wait()
    wide = jnp.concatenate([noise_raw[m].astype(F32) for m in range(MEMBERS)], axis=0)
    for c in range(COL):
        noise[c] = wide[:, c * FEAT : (c + 1) * FEAT].astype(BF16)

    for k, device, slot in ((0, right, 3), (1, left, 1), (0, pair, 4), (1, right, 3), (0, left, 1), (1, pair, 4)):
        b_send(0, k, slot, device)

    def a_at(slot):
        return abuf.at[:, pl.ds(slot * PART, PART), :]

    target = (ylo + mine // NX) % 2 * NX + (x + NX - mine % NX) % NX
    fetch = pltpu.make_async_remote_copy(
        src_ref=noise.at[pl.ds(2 * target, 2)],
        dst_ref=a_at(mine),
        send_sem=lsem.at[4],
        recv_sem=asem.at[0],
        device_id=(target, col),
        device_id_type=MESH,
    )
    keep = pltpu.make_async_copy(noise.at[pl.ds(2 * pop, 2)], a_at(0), lsem.at[5])

    @pl.when(mine > 0)
    def _():
        fetch.start()

    @pl.when(mine == 0)
    def _():
        keep.start()

    x_send(col, None, 2, far, acts)
    own_pieces(2, 4)

    c_down, c_up = col_at(3, 0, 0), col_at(1, 0, 0)
    c_far, c_opp = col_at(0, 1, 0), col_at(2, 0, 0)
    f_down, f_up, f_opp = col_at(3, 1, 0), col_at(1, 1, 0), col_at(2, 1, 0)

    def add_low(c):
        low[...] += lax.dot_general(
            xbuf[c],
            noise[c],
            (((1,), (1,)), ((), ())),
            preferred_element_type=F32,
        )

    def relay(first, last):
        for j in range(first, last):
            w_arrive(3, 0, j)
            w_send(3, 0, j, 2, right)
            w_arrive(1, 1, j)
            w_send(1, 1, j, 2, left)

    def across(first, last):
        for j in range(first, last):
            for h in range(2):
                w_arrive(2, h, j)
                w_send(2, h, j, 6, pair)

    def pass_on(first, last):
        for i in range(first, last):
            h, j = to_pair[i]
            w_arrive(4, h, j)
            w_send(4, h, j, 7, right)
            w_send(4, h, j, 5, left)

    b_arrive(3, 0)
    b_send(3, 0, 2, right)
    b_arrive(1, 1)
    b_send(1, 1, 2, left)
    for k in range(2):
        b_arrive(4, k)
        b_send(4, k, 7, right)
        b_send(4, k, 5, left)
    own_pieces(4, 7)

    low[...] = jnp.zeros_like(low)
    own_acts.wait()
    add_low(col)

    x_arrive(c_down, None, 0)
    x_send(c_down, 0, 5, up)
    x_send(c_down, None, 10, twin)
    x_arrive(c_up, None, 1)
    x_send(c_up, 1, 6, down)
    x_send(c_up, None, 11, twin)

    @pl.when(mine > 0)
    def _():
        fetch.wait()

    @pl.when(mine == 0)
    def _():
        keep.wait()

    for dz, device in ((1, up), (3, down), (2, (pop, col_at(2, 0, 0)))):
        send(a_at(mine), a_at(mine), asem.at[2 * dz], device)
    send(a_at(mine), a_at(mine), asem.at[1], twin)

    for k in range(2):
        b_arrive(2, k)
        b_send(2, k, 6, pair)
    own_to_pair(1, 5)
    add_low(c_down)
    add_low(c_up)
    x_arrive(c_far, None, 2)
    x_send(c_far, None, 3, up)
    x_send(c_far, None, 4, down)
    x_send(c_far, None, 12, twin)
    own_pieces(7, 9)
    add_low(c_far)

    b_arrive(3, 1)
    b_arrive(1, 0)
    for slot in (7, 5, 6):
        for k in range(2):
            b_arrive(slot, k)
    def owner(dz, dc):
        return ((z + NZ - dz) % NZ) * 2 + (core * (1 - 2 * dc) + dc)

    for dz in (1, 3, 2):
        block = a_at(owner(dz, 0))
        arrive(block, asem.at[2 * dz])
        send(block, block, asem.at[2 * dz + 1], twin)
    for dz in range(NZ):
        arrive(a_at(owner(dz, 1)), asem.at[2 * dz + 1])

    @pl.loop(1, POP)
    def _(slot):
        packed = tbuf[slot].astype(F32)
        for g in range(4):
            mid = packed[:, g * REST : (g + 1) * REST].astype(BF16)
            wbuf[slot, pl.ds(g * 112, 112), pl.ds(MAIN, REST)] = mid[:112]
            bbuf[
                pl.ds(pl.multiple_of(slot * PART + g * 16, 16), 16), pl.ds(MAIN, REST)
            ] = mid[112:]

    squares = jnp.zeros((), F32)
    for h in range(2):
        block = lax.dot_general(
            abuf[h], bbuf[...], (((0,), (0,)), ((), ())), preferred_element_type=F32
        )
        delta[pl.ds(h * FEAT, FEAT), :] = block
        squares += jnp.sum(block * block)
    part[0] = jnp.full((8, 128), squares, F32)

    for i, device in pop_peers:
        send(part.at[0], parts.at[8 + i], rsem.at[8 + i], device)
    own_pieces(9, 10)
    own_to_pair(5, 8)
    relay(0, NG)
    x_arrive(c_opp, 0, 5)
    x_send(c_opp, 0, 15, twin)
    x_arrive(c_opp, 1, 6)
    x_send(c_opp, 1, 16, twin)
    add_low(c_opp)
    x_arrive(f_down, None, 3)
    x_send(f_down, 0, 7, up)
    x_send(f_down, None, 13, twin)
    x_arrive(f_up, None, 4)
    x_send(f_up, 1, 8, down)
    x_send(f_up, None, 14, twin)
    total = part[0]
    for i, _ in pop_peers:
        arrive(parts.at[8 + i], rsem.at[8 + i])
        total = total + parts[8 + i]
    part[1] = total
    add_low(f_down)
    add_low(f_up)
    send(part.at[1], parts.at[8], rsem.at[8], far)
    own_to_pair(8, 10)
    across(0, 1)
    pass_on(0, 4)

    def add_twin(dz, dy, *sems):
        c = col_at(dz, dy, 1)
        for i, sem in enumerate(sems):
            x_arrive(c, i if len(sems) > 1 else None, sem)
        add_low(c)

    add_twin(0, 0, 9)
    add_twin(3, 0, 10)
    across(1, 2)
    add_twin(1, 0, 11)
    add_twin(0, 1, 12)
    arrive(parts.at[8], rsem.at[8])
    part[2] = part[1] + parts[8]
    add_twin(2, 0, 15, 16)
    across(2, 3)
    for i, device in col_peers:
        send(part.at[2], parts.at[i], rsem.at[i], device)
    x_arrive(f_opp, 0, 7)
    x_send(f_opp, 0, 17, twin)
    x_arrive(f_opp, 1, 8)
    x_send(f_opp, 1, 18, twin)
    add_low(f_opp)
    add_twin(3, 1, 13)
    add_twin(1, 1, 14)
    across(3, 4)
    add_twin(2, 1, 17, 18)
    pass_on(4, 5)
    across(4, NG)

    rank = lax.broadcasted_iota(jnp.int32, (TOKENS, PART), 1) // 4
    token = lax.broadcasted_iota(jnp.int32, (TOKENS, PART), 0) // 64
    low[...] = jnp.where(rank == token, low[...] * 0.5, 0.0)

    def rows(i):
        return pl.ds(pl.multiple_of(i * TILE, TILE), TILE)

    @pl.loop(0, TOKENS // TILE)
    def _(i):
        left_over = low[rows(i), :]
        value = None
        for _ in range(3):
            term = left_over.astype(BF16)
            left_over = left_over - term.astype(F32)
            product = jnp.dot(term, out_noise[...], preferred_element_type=F32)
            value = product if value is None else value + product
        acc[rows(i), :] = value

    pass_on(5, 6)

    def dot(i, slot, h, cols):
        c = 2 * pop_at(slot // NX, slot % NX) + h
        return jnp.dot(
            xbuf[c, rows(i), :],
            wbuf[slot, pl.ds(h * FEAT, FEAT), cols],
            preferred_element_type=F32,
        )

    everything = pl.ds(0, WIDE)

    def blocks(slot):
        @pl.loop(0, TOKENS // TILE)
        def _(i):
            for h in range(2):
                acc[rows(i), :] += dot(i, slot, h, everything)

    blocks(0)
    pass_on(6, 7)
    for j in range(NG):
        w_arrive(3, 1, j)
        w_arrive(1, 0, j)
    blocks(1)
    pass_on(7, 9)
    blocks(3)
    pass_on(9, 10)
    blocks(4)
    blocks(2)

    total = part[2]
    for i, _ in col_peers:
        arrive(parts.at[i], rsem.at[i])
        total = total + parts[i]
    scale = lax.rsqrt(total / (D * F) + 1e-06)[0:1, 0:1]
    step = delta[...] * scale
    step_out[...] = step
    new_out[...] = (wbuf[0].astype(F32) + 0.01 * step).astype(BF16)
    for j in range(NG):
        for h in range(2):
            for slot in (5, 7, 6):
                w_arrive(slot, h, j)
        first, n = GROUPS[j]
        cols = pl.ds(first, n if j < NG - 1 else WIDE - first)

        @pl.loop(0, TOKENS // TILE)
        def _(i):
            value = acc[rows(i), cols]
            for slot in (5, 7, 6):
                for h in range(2):
                    value = value + dot(i, slot, h, cols)
            out[rows(i), cols] = value.astype(BF16)


    for copy in sent:
        copy.wait_send()


def put_out(out_v, step_v, new_v, out, step_out, new_out, sem):
    writes = [
        pltpu.make_async_copy(src, dst, sem.at[i])
        for i, (src, dst) in enumerate(
            ((step_v, step_out), (out_v, out), (new_v, new_out))
        )
    ]
    for copy in writes:
        copy.start()
    for copy in writes:
        copy.wait()


def body(acts, weight, input_noise_factor, output_noise_factor, ranks):
    hbm = pl.BlockSpec(memory_space=pltpu.HBM)
    vmem = pl.BlockSpec(memory_space=pltpu.VMEM)
    made = pl.pallas_call(
        kernel,
        out_shape=(
            pltpu.VMEM((TOKENS, WIDE), BF16),
            pltpu.VMEM((ROWS, WIDE), F32),
            pltpu.VMEM((ROWS, WIDE), BF16),
        ),
        in_specs=[hbm] * 5,
        out_specs=(vmem,) * 3,
        scratch_shapes=[
            pltpu.VMEM((POP, ROWS, WIDE), BF16),
            pltpu.VMEM((COL, TOKENS, FEAT), BF16),
            pltpu.VMEM((2, POP * PART, FEAT), BF16),
            pltpu.VMEM((POP * PART, WIDE), BF16),
            pltpu.VMEM((POP, 128, 128), BF16),
            pltpu.SMEM((MEMBERS,), jnp.int32),
            pltpu.VMEM((MEMBERS, 4, D), BF16),
            pltpu.VMEM((MEMBERS, 4, WIDE), BF16),
            pltpu.VMEM((COL, PART, FEAT), BF16),
            pltpu.VMEM((PART, WIDE), BF16),
            pltpu.VMEM((TOKENS, WIDE), F32),
            pltpu.VMEM((TOKENS, PART), F32),
            pltpu.VMEM((ROWS, WIDE), F32),
            pltpu.VMEM((3, 8, 128), F32),
            pltpu.VMEM((16, 8, 128), F32),
            pltpu.SemaphoreType.DMA((POP * 2 * NG,)),
            pltpu.SemaphoreType.DMA((POP * 2,)),
            pltpu.SemaphoreType.DMA((POP * 2,)),
            pltpu.SemaphoreType.DMA((8,)),
            pltpu.SemaphoreType.DMA((19,)),
            pltpu.SemaphoreType.DMA((16,)),
            pltpu.SemaphoreType.DMA((192,)),
            pltpu.SemaphoreType.DMA((13,)),
        ],
        compiler_params=pltpu.CompilerParams(
            collective_id=0, has_side_effects=True, vmem_limit_bytes=57 * 1024 * 1024
        ),
    )(
        acts.reshape(TOKENS, FEAT),
        weight,
        input_noise_factor,
        output_noise_factor,
        pltpu.with_memory_space_constraint(ranks, pltpu.HBM),
    )
    out, step_dir, new_weight = pl.pallas_call(
        put_out,
        out_shape=(
            jax.ShapeDtypeStruct((TOKENS, WIDE), BF16),
            jax.ShapeDtypeStruct((ROWS, WIDE), F32),
            jax.ShapeDtypeStruct((ROWS, WIDE), BF16),
        ),
        in_specs=[vmem] * 3,
        out_specs=(hbm,) * 3,
        scratch_shapes=[pltpu.SemaphoreType.DMA((3,))],
        compiler_params=pltpu.CompilerParams(vmem_limit_bytes=16 * 1024 * 1024),
    )(*made)
    return (out.reshape(MEMBERS, TOKENS // MEMBERS, WIDE), step_dir, new_weight)


def solution(mesh):
    in_specs = (
        P("pop", None, "col"),
        P("pop", "col"),
        P("pop", None, None),
        P("pop", None, "col"),
        P("pop"),
    )
    out_specs = (P("pop", None, "col"), P("pop", "col"), P("pop", "col"))
    return jax.shard_map(body, mesh=mesh, in_specs=in_specs, out_specs=out_specs, check_vma=False)
```

```python
import jax
import jax.numpy as jnp
from jax import lax
from jax.experimental import pallas as pl
from jax.experimental.pallas import tpu as pltpu
from jax.sharding import PartitionSpec as P

D = 3584
F = 18944
NX = 4
NZ = 4
POP = 8
COL = 16
MEMBERS = 16
ROWS = 448
WIDE = 1184
MAIN = 1152
REST = WIDE - MAIN
FEAT = 224
TOKENS = 1024
PART = 64
GROUPS = ((0, 256), (256, 256), (512, 256), (768, 256), (1024, 128))
NG = len(GROUPS)
TILE = 256
MESH = pl.DeviceIdType.MESH
BF16 = jnp.bfloat16
F32 = jnp.float32


def kernel(
    acts,
    weight,
    noise_in,
    out_in,
    ranks_in,
    out,
    step_out,
    new_out,
    wbuf,
    xbuf,
    acc,
    abuf,
    bbuf,
    tbuf,
    ranks,
    noise_raw,
    out_raw,
    noise,
    out_noise,
    low,
    delta,
    part,
    parts,
    wsem,
    bsem,
    tsem,
    asem,
    xsem,
    rsem,
    ssem,
    lsem,
):
    pop, col = lax.axis_index("pop"), lax.axis_index("col")
    x, ylo = pop % NX, pop // NX
    z, yhi, core = col // 4, (col // 2) % 2, col % 2
    mine = z * 2 + core

    def pop_at(dy, dx):
        return (ylo * (1 - 2 * dy) + dy) * NX + (x + dx) % NX

    def col_at(dz, dy, dc):
        return (
            ((z + dz) % NZ) * 4
            + (yhi * (1 - 2 * dy) + dy) * 2
            + (core * (1 - 2 * dc) + dc)
        )

    right, left = (pop_at(0, 1), col), (pop_at(0, 3), col)
    pair = (pop_at(1, 0), col)
    up, down = (pop, col_at(1, 0, 0)), (pop, col_at(3, 0, 0))
    far, twin = (pop, col_at(0, 1, 0)), (pop, col_at(0, 0, 1))
    pop_peers = [
        (dy * NX + dx, (pop_at(dy, dx), col))
        for dy in range(2)
        for dx in range(NX)
        if dy + dx > 0
    ]
    col_peers = [
        (dz * 2 + dc, (pop, col_at(dz, 0, dc)))
        for dz in range(NZ)
        for dc in range(2)
        if dz + dc > 0
    ]

    sent = []

    def send(src, dst, sem, device):
        copy = pltpu.make_async_remote_copy(
            src_ref=src,
            dst_ref=dst,
            send_sem=ssem.at[len(sent)],
            recv_sem=sem,
            device_id=device,
            device_id_type=MESH,
        )
        copy.start()
        sent.append(copy)

    def arrive(dst, sem):
        pltpu.make_async_remote_copy(
            src_ref=dst,
            dst_ref=dst,
            send_sem=ssem.at[0],
            recv_sem=sem,
            device_id=right,
            device_id_type=MESH,
        ).wait_recv()

    own_noise = pltpu.make_async_copy(noise_in, noise_raw, lsem.at[0])
    own_out = pltpu.make_async_copy(out_in, out_raw, lsem.at[1])
    own_weight = pltpu.make_async_copy(weight, wbuf.at[0], lsem.at[2])
    own_acts = pltpu.make_async_copy(acts, xbuf.at[col], lsem.at[3])
    own_ranks = pltpu.make_async_copy(ranks_in, ranks, lsem.at[6])
    for copy in (own_ranks, own_out, own_noise, own_weight, own_acts):
        copy.start()

    barrier = pltpu.get_barrier_semaphore()
    peers = [device for _, device in pop_peers + col_peers] + [far]
    for device in peers:
        pl.semaphore_signal(barrier, inc=1, device_id=device, device_id_type=MESH)
    pl.semaphore_wait(barrier, len(peers))

    def piece(h, j):
        return pl.ds(h * FEAT, FEAT), pl.ds(*GROUPS[j])

    def w_at(slot, h, j):
        r, c = piece(h, j)
        return wbuf.at[slot, r, c]

    def w_send(src_slot, h, j, dst_slot, device):
        r, c = piece(h, j)
        src = weight.at[r, c] if src_slot == 0 else wbuf.at[src_slot, r, c]
        send(src, w_at(dst_slot, h, j), wsem.at[(dst_slot * 2 + h) * NG + j], device)

    def w_arrive(slot, h, j):
        arrive(w_at(slot, h, j), wsem.at[(slot * 2 + h) * NG + j])

    def b_at(slot, k):
        return bbuf.at[pl.ds(slot * PART + k * 32, 32), pl.ds(0, MAIN)]

    def t_at(slot, k):
        return tbuf.at[slot, pl.ds(k * 64, 64), :]

    def b_send(src_slot, k, dst_slot, device):
        send(b_at(src_slot, k), b_at(dst_slot, k), bsem.at[dst_slot * 2 + k], device)
        send(t_at(src_slot, k), t_at(dst_slot, k), tsem.at[dst_slot * 2 + k], device)

    def b_arrive(slot, k):
        arrive(b_at(slot, k), bsem.at[slot * 2 + k])
        arrive(t_at(slot, k), tsem.at[slot * 2 + k])

    def x_at(c, half=None):
        if half is None:
            return xbuf.at[c]
        return xbuf.at[c, pl.ds(half * (TOKENS // 2), TOKENS // 2), :]

    def x_send(c, half, sem, device, src=None):
        send(x_at(c, half) if src is None else src, x_at(c, half), xsem.at[sem], device)

    def x_arrive(c, half, sem):
        arrive(x_at(c, half), xsem.at[sem])

    to_right = [(h, j) for h in (0, 1) for j in range(NG)]
    to_left = [(h, j) for h in (1, 0) for j in range(NG)]
    to_pair = [(h, j) for j in range(NG) for h in (0, 1)]

    def own_pieces(first, last):
        for i in range(first, last):
            w_send(0, *to_right[i], 3, right)
            w_send(0, *to_left[i], 1, left)

    def own_to_pair(first, last):
        for i in range(first, last):
            w_send(0, *to_pair[i], 4, pair)

    x_send(col, None, 0, up, acts)
    x_send(col, None, 1, down, acts)
    own_pieces(0, 2)
    own_to_pair(0, 1)
    x_send(col, None, 9, twin, acts)

    own_ranks.wait()
    own_out.wait()
    raw = jnp.concatenate([out_raw[m].astype(F32) for m in range(MEMBERS)], axis=0)
    out_noise[...] = raw.astype(BF16)
    fit = jnp.concatenate(
        [
            jnp.full((4, 1), ranks[m].astype(F32), F32) / (MEMBERS * POP - 1) - 0.5
            for m in range(MEMBERS)
        ],
        axis=0,
    )
    scaled = raw * fit
    bbuf[pl.ds(0, PART), :] = scaled.astype(BF16)
    own_weight.wait()
    last = wbuf[0, :, pl.ds(MAIN, REST)].astype(F32)
    tbuf[0, pl.ds(0, 112), :] = jnp.concatenate(
        [last[g * 112 : g * 112 + 112] for g in range(4)], axis=1
    ).astype(BF16)
    tbuf[0, pl.ds(112, 16), :] = jnp.concatenate(
        [scaled[g * 16 : g * 16 + 16, MAIN:WIDE] for g in range(4)], axis=1
    ).astype(BF16)
    own_noise.wait()
    wide = jnp.concatenate([noise_raw[m].astype(F32) for m in range(MEMBERS)], axis=0)
    for c in range(COL):
        noise[c] = wide[:, c * FEAT : (c + 1) * FEAT].astype(BF16)

    for k, device, slot in ((0, right, 3), (1, left, 1), (0, pair, 4), (1, right, 3), (0, left, 1), (1, pair, 4)):
        b_send(0, k, slot, device)

    def a_at(slot):
        return abuf.at[:, pl.ds(slot * PART, PART), :]

    target = (ylo + mine // NX) % 2 * NX + (x + NX - mine % NX) % NX
    fetch = pltpu.make_async_remote_copy(
        src_ref=noise.at[pl.ds(2 * target, 2)],
        dst_ref=a_at(mine),
        send_sem=lsem.at[4],
        recv_sem=asem.at[0],
        device_id=(target, col),
        device_id_type=MESH,
    )
    keep = pltpu.make_async_copy(noise.at[pl.ds(2 * pop, 2)], a_at(0), lsem.at[5])

    @pl.when(mine > 0)
    def _():
        fetch.start()

    @pl.when(mine == 0)
    def _():
        keep.start()

    x_send(col, None, 2, far, acts)
    own_pieces(2, 4)

    c_down, c_up = col_at(3, 0, 0), col_at(1, 0, 0)
    c_far, c_opp = col_at(0, 1, 0), col_at(2, 0, 0)
    f_down, f_up, f_opp = col_at(3, 1, 0), col_at(1, 1, 0), col_at(2, 1, 0)

    def add_low(c):
        low[...] += lax.dot_general(
            xbuf[c],
            noise[c],
            (((1,), (1,)), ((), ())),
            preferred_element_type=F32,
        )

    def relay(first, last):
        for j in range(first, last):
            w_arrive(3, 0, j)
            w_send(3, 0, j, 2, right)
            w_arrive(1, 1, j)
            w_send(1, 1, j, 2, left)

    def across(first, last):
        for j in range(first, last):
            for h in range(2):
                w_arrive(2, h, j)
                w_send(2, h, j, 6, pair)

    def pass_on(first, last):
        for i in range(first, last):
            h, j = to_pair[i]
            w_arrive(4, h, j)
            w_send(4, h, j, 7, right)
            w_send(4, h, j, 5, left)

    b_arrive(3, 0)
    b_send(3, 0, 2, right)
    b_arrive(1, 1)
    b_send(1, 1, 2, left)
    for k in range(2):
        b_arrive(4, k)
        b_send(4, k, 7, right)
        b_send(4, k, 5, left)
    own_pieces(4, 7)

    low[...] = jnp.zeros_like(low)
    own_acts.wait()
    add_low(col)

    x_arrive(c_down, None, 0)
    x_send(c_down, 0, 5, up)
    x_send(c_down, None, 10, twin)
    x_arrive(c_up, None, 1)
    x_send(c_up, 1, 6, down)
    x_send(c_up, None, 11, twin)

    @pl.when(mine > 0)
    def _():
        fetch.wait()

    @pl.when(mine == 0)
    def _():
        keep.wait()

    for dz, device in ((1, up), (3, down), (2, (pop, col_at(2, 0, 0)))):
        send(a_at(mine), a_at(mine), asem.at[2 * dz], device)
    send(a_at(mine), a_at(mine), asem.at[1], twin)

    for k in range(2):
        b_arrive(2, k)
        b_send(2, k, 6, pair)
    own_to_pair(1, 5)
    add_low(c_down)
    add_low(c_up)
    x_arrive(c_far, None, 2)
    x_send(c_far, None, 3, up)
    x_send(c_far, None, 4, down)
    x_send(c_far, None, 12, twin)
    own_pieces(7, 9)
    add_low(c_far)

    b_arrive(3, 1)
    b_arrive(1, 0)
    for slot in (7, 5, 6):
        for k in range(2):
            b_arrive(slot, k)
    def owner(dz, dc):
        return ((z + NZ - dz) % NZ) * 2 + (core * (1 - 2 * dc) + dc)

    for dz in (1, 3, 2):
        block = a_at(owner(dz, 0))
        arrive(block, asem.at[2 * dz])
        send(block, block, asem.at[2 * dz + 1], twin)
    for dz in range(NZ):
        arrive(a_at(owner(dz, 1)), asem.at[2 * dz + 1])

    @pl.loop(1, POP)
    def _(slot):
        packed = tbuf[slot].astype(F32)
        for g in range(4):
            mid = packed[:, g * REST : (g + 1) * REST].astype(BF16)
            wbuf[slot, pl.ds(g * 112, 112), pl.ds(MAIN, REST)] = mid[:112]
            bbuf[
                pl.ds(pl.multiple_of(slot * PART + g * 16, 16), 16), pl.ds(MAIN, REST)
            ] = mid[112:]

    squares = jnp.zeros((), F32)
    for h in range(2):
        block = lax.dot_general(
            abuf[h], bbuf[...], (((0,), (0,)), ((), ())), preferred_element_type=F32
        )
        delta[pl.ds(h * FEAT, FEAT), :] = block
        squares += jnp.sum(block * block)
    part[0] = jnp.full((8, 128), squares, F32)

    for i, device in pop_peers:
        send(part.at[0], parts.at[8 + i], rsem.at[8 + i], device)
    own_pieces(9, 10)
    own_to_pair(5, 8)
    relay(0, NG)
    x_arrive(c_opp, 0, 5)
    x_send(c_opp, 0, 15, twin)
    x_arrive(c_opp, 1, 6)
    x_send(c_opp, 1, 16, twin)
    add_low(c_opp)
    x_arrive(f_down, None, 3)
    x_send(f_down, 0, 7, up)
    x_send(f_down, None, 13, twin)
    x_arrive(f_up, None, 4)
    x_send(f_up, 1, 8, down)
    x_send(f_up, None, 14, twin)
    total = part[0]
    for i, _ in pop_peers:
        arrive(parts.at[8 + i], rsem.at[8 + i])
        total = total + parts[8 + i]
    part[1] = total
    add_low(f_down)
    add_low(f_up)
    send(part.at[1], parts.at[8], rsem.at[8], far)
    own_to_pair(8, 10)
    across(0, 1)
    pass_on(0, 4)

    def add_twin(dz, dy, *sems):
        c = col_at(dz, dy, 1)
        for i, sem in enumerate(sems):
            x_arrive(c, i if len(sems) > 1 else None, sem)
        add_low(c)

    add_twin(0, 0, 9)
    add_twin(3, 0, 10)
    across(1, 2)
    add_twin(1, 0, 11)
    add_twin(0, 1, 12)
    arrive(parts.at[8], rsem.at[8])
    part[2] = part[1] + parts[8]
    add_twin(2, 0, 15, 16)
    across(2, 3)
    for i, device in col_peers:
        send(part.at[2], parts.at[i], rsem.at[i], device)
    x_arrive(f_opp, 0, 7)
    x_send(f_opp, 0, 17, twin)
    x_arrive(f_opp, 1, 8)
    x_send(f_opp, 1, 18, twin)
    add_low(f_opp)
    add_twin(3, 1, 13)
    add_twin(1, 1, 14)
    across(3, 4)
    add_twin(2, 1, 17, 18)
    pass_on(4, 5)
    across(4, NG)

    rank = lax.broadcasted_iota(jnp.int32, (TOKENS, PART), 1) // 4
    token = lax.broadcasted_iota(jnp.int32, (TOKENS, PART), 0) // 64
    low[...] = jnp.where(rank == token, low[...] * 0.5, 0.0)

    def rows(i):
        return pl.ds(pl.multiple_of(i * TILE, TILE), TILE)

    @pl.loop(0, TOKENS // TILE)
    def _(i):
        left_over = low[rows(i), :]
        value = None
        for _ in range(3):
            term = left_over.astype(BF16)
            left_over = left_over - term.astype(F32)
            product = jnp.dot(term, out_noise[...], preferred_element_type=F32)
            value = product if value is None else value + product
        acc[rows(i), :] = value

    pass_on(5, 6)

    def dot(i, slot, h, cols):
        c = 2 * pop_at(slot // NX, slot % NX) + h
        return jnp.dot(
            xbuf[c, rows(i), :],
            wbuf[slot, pl.ds(h * FEAT, FEAT), cols],
            preferred_element_type=F32,
        )

    everything = pl.ds(0, WIDE)

    def blocks(slot):
        @pl.loop(0, TOKENS // TILE)
        def _(i):
            for h in range(2):
                acc[rows(i), :] += dot(i, slot, h, everything)

    blocks(0)
    pass_on(6, 7)
    for j in range(NG):
        w_arrive(3, 1, j)
        w_arrive(1, 0, j)
    blocks(1)
    pass_on(7, 9)
    blocks(3)
    pass_on(9, 10)
    blocks(4)
    blocks(2)

    total = part[2]
    for i, _ in col_peers:
        arrive(parts.at[i], rsem.at[i])
        total = total + parts[i]
    scale = lax.rsqrt(total / (D * F) + 1e-06)[0:1, 0:1]
    step = delta[...] * scale
    step_out[...] = step
    new_out[...] = (wbuf[0].astype(F32) + 0.01 * step).astype(BF16)
    for j in range(NG):
        for h in range(2):
            for slot in (5, 7, 6):
                w_arrive(slot, h, j)
        if j == NG - 1:
            break
        cols = pl.ds(*GROUPS[j])

        @pl.loop(0, TOKENS // TILE)
        def _(i):
            value = acc[rows(i), cols]
            for slot in (5, 7, 6):
                for h in range(2):
                    value = value + dot(i, slot, h, cols)
            out[rows(i), cols] = value.astype(BF16)


    for copy in sent:
        copy.wait_send()


def put_out(
    out_v, step_v, new_v, wbuf, xbuf, acc, out, step_out, new_out, last, sem
):
    first = GROUPS[-1][0]
    cols = pl.ds(first, WIDE - first)
    ready = pl.ds(0, first)
    pairs = (
        (step_v, step_out),
        (out_v.at[:, ready], out.at[:, ready]),
        (new_v, new_out),
        (last, out.at[:, cols]),
    )
    writes = [
        pltpu.make_async_copy(src, dst, sem.at[i]) for i, (src, dst) in enumerate(pairs)
    ]
    for copy in writes[:3]:
        copy.start()
    pop = lax.axis_index("pop")
    x, ylo = pop % NX, pop // NX

    @pl.loop(0, TOKENS // TILE)
    def _(i):
        rows = pl.ds(pl.multiple_of(i * TILE, TILE), TILE)
        value = acc[rows, cols]
        for slot in (5, 7, 6):
            source = (1 - ylo) * NX + (x + slot % NX) % NX
            for h in range(2):
                value = value + jnp.dot(
                    xbuf[2 * source + h, rows, :],
                    wbuf[slot, pl.ds(h * FEAT, FEAT), cols],
                    preferred_element_type=F32,
                )
        last[rows, :] = value.astype(BF16)

    writes[3].start()
    for copy in writes:
        copy.wait()


def body(acts, weight, input_noise_factor, output_noise_factor, ranks):
    hbm = pl.BlockSpec(memory_space=pltpu.HBM)
    vmem = pl.BlockSpec(memory_space=pltpu.VMEM)
    made = pl.pallas_call(
        kernel,
        out_shape=(
            pltpu.VMEM((TOKENS, WIDE), BF16),
            pltpu.VMEM((ROWS, WIDE), F32),
            pltpu.VMEM((ROWS, WIDE), BF16),
            pltpu.VMEM((POP, ROWS, WIDE), BF16),
            pltpu.VMEM((COL, TOKENS, FEAT), BF16),
            pltpu.VMEM((TOKENS, WIDE), F32),
        ),
        in_specs=[hbm] * 5,
        out_specs=(vmem,) * 6,
        scratch_shapes=[
            pltpu.VMEM((2, POP * PART, FEAT), BF16),
            pltpu.VMEM((POP * PART, WIDE), BF16),
            pltpu.VMEM((POP, 128, 128), BF16),
            pltpu.SMEM((MEMBERS,), jnp.int32),
            pltpu.VMEM((MEMBERS, 4, D), BF16),
            pltpu.VMEM((MEMBERS, 4, WIDE), BF16),
            pltpu.VMEM((COL, PART, FEAT), BF16),
            pltpu.VMEM((PART, WIDE), BF16),
            pltpu.VMEM((TOKENS, PART), F32),
            pltpu.VMEM((ROWS, WIDE), F32),
            pltpu.VMEM((3, 8, 128), F32),
            pltpu.VMEM((16, 8, 128), F32),
            pltpu.SemaphoreType.DMA((POP * 2 * NG,)),
            pltpu.SemaphoreType.DMA((POP * 2,)),
            pltpu.SemaphoreType.DMA((POP * 2,)),
            pltpu.SemaphoreType.DMA((8,)),
            pltpu.SemaphoreType.DMA((19,)),
            pltpu.SemaphoreType.DMA((16,)),
            pltpu.SemaphoreType.DMA((192,)),
            pltpu.SemaphoreType.DMA((13,)),
        ],
        compiler_params=pltpu.CompilerParams(
            collective_id=0, has_side_effects=True, vmem_limit_bytes=34 * 1024 * 1024
        ),
    )(
        acts.reshape(TOKENS, FEAT),
        weight,
        input_noise_factor,
        output_noise_factor,
        pltpu.with_memory_space_constraint(ranks, pltpu.HBM),
    )
    out, step_dir, new_weight = pl.pallas_call(
        put_out,
        out_shape=(
            jax.ShapeDtypeStruct((TOKENS, WIDE), BF16),
            jax.ShapeDtypeStruct((ROWS, WIDE), F32),
            jax.ShapeDtypeStruct((ROWS, WIDE), BF16),
        ),
        in_specs=[vmem] * 6,
        out_specs=(hbm,) * 3,
        scratch_shapes=[
            pltpu.VMEM((TOKENS, WIDE - GROUPS[-1][0]), BF16),
            pltpu.SemaphoreType.DMA((4,)),
        ],
        compiler_params=pltpu.CompilerParams(vmem_limit_bytes=4 * 1024 * 1024),
    )(*made)
    return (out.reshape(MEMBERS, TOKENS // MEMBERS, WIDE), step_dir, new_weight)


def solution(mesh):
    in_specs = (
        P("pop", None, "col"),
        P("pop", "col"),
        P("pop", None, None),
        P("pop", None, "col"),
        P("pop"),
    )
    out_specs = (P("pop", None, "col"), P("pop", "col"), P("pop", "col"))
    return jax.shard_map(body, mesh=mesh, in_specs=in_specs, out_specs=out_specs, check_vma=False)
```

```python
import jax
import jax.numpy as jnp
from jax import lax
from jax.experimental import pallas as pl
from jax.experimental.pallas import tpu as pltpu
from jax.sharding import PartitionSpec as P

D = 3584
F = 18944
NX = 4
NZ = 4
POP = 8
COL = 16
MEMBERS = 16
ROWS = 448
WIDE = 1184
MAIN = 1152
REST = WIDE - MAIN
FEAT = 224
TOKENS = 1024
PART = 64
GROUPS = ((0, 256), (256, 256), (512, 256), (768, 256), (1024, 128))
NG = len(GROUPS)
TILE = 256
MESH = pl.DeviceIdType.MESH
BF16 = jnp.bfloat16
F32 = jnp.float32


def kernel(
    acts,
    weight,
    noise_in,
    out_in,
    ranks_in,
    out,
    step_out,
    new_out,
    wbuf,
    xbuf,
    acc,
    abuf,
    bbuf,
    tbuf,
    ranks,
    noise_raw,
    out_raw,
    noise,
    out_noise,
    low,
    delta,
    part,
    parts,
    wsem,
    bsem,
    tsem,
    asem,
    esem,
    xsem,
    rsem,
    ssem,
    lsem,
):
    pop, col = lax.axis_index("pop"), lax.axis_index("col")
    x, ylo = pop % NX, pop // NX
    z, yhi, core = col // 4, (col // 2) % 2, col % 2
    mine = z * 2 + core

    def pop_at(dy, dx):
        return (ylo * (1 - 2 * dy) + dy) * NX + (x + dx) % NX

    def col_at(dz, dy, dc):
        return (
            ((z + dz) % NZ) * 4
            + (yhi * (1 - 2 * dy) + dy) * 2
            + (core * (1 - 2 * dc) + dc)
        )

    right, left = (pop_at(0, 1), col), (pop_at(0, 3), col)
    pair = (pop_at(1, 0), col)
    up, down = (pop, col_at(1, 0, 0)), (pop, col_at(3, 0, 0))
    far, twin = (pop, col_at(0, 1, 0)), (pop, col_at(0, 0, 1))
    pop_peers = [
        (dy * NX + dx, (pop_at(dy, dx), col))
        for dy in range(2)
        for dx in range(NX)
        if dy + dx > 0
    ]
    col_peers = [
        (dz * 2 + dc, (pop, col_at(dz, 0, dc)))
        for dz in range(NZ)
        for dc in range(2)
        if dz + dc > 0
    ]

    sent = []

    def send(src, dst, sem, device):
        copy = pltpu.make_async_remote_copy(
            src_ref=src,
            dst_ref=dst,
            send_sem=ssem.at[len(sent)],
            recv_sem=sem,
            device_id=device,
            device_id_type=MESH,
        )
        copy.start()
        sent.append(copy)

    def arrive(dst, sem):
        pltpu.make_async_remote_copy(
            src_ref=dst,
            dst_ref=dst,
            send_sem=ssem.at[0],
            recv_sem=sem,
            device_id=right,
            device_id_type=MESH,
        ).wait_recv()

    barrier = pltpu.get_barrier_semaphore()
    peers = [device for _, device in pop_peers + col_peers] + [far]
    for device in peers:
        pl.semaphore_signal(barrier, inc=1, device_id=device, device_id_type=MESH)
    own_noise = pltpu.make_async_copy(noise_in, noise_raw, lsem.at[0])
    own_out = pltpu.make_async_copy(out_in, out_raw, lsem.at[1])
    own_weight = pltpu.make_async_copy(weight, wbuf.at[0], lsem.at[2])
    own_acts = pltpu.make_async_copy(acts, xbuf.at[col], lsem.at[3])
    own_ranks = pltpu.make_async_copy(ranks_in, ranks, lsem.at[6])
    for copy in (own_ranks, own_out, own_noise, own_weight, own_acts):
        copy.start()

    pl.semaphore_wait(barrier, len(peers))

    def piece(h, j):
        return pl.ds(h * FEAT, FEAT), pl.ds(*GROUPS[j])

    def w_at(slot, h, j):
        r, c = piece(h, j)
        return wbuf.at[slot, r, c]

    def w_send(src_slot, h, j, dst_slot, device):
        r, c = piece(h, j)
        src = weight.at[r, c] if src_slot == 0 else wbuf.at[src_slot, r, c]
        send(src, w_at(dst_slot, h, j), wsem.at[(dst_slot * 2 + h) * NG + j], device)

    def w_arrive(slot, h, j):
        arrive(w_at(slot, h, j), wsem.at[(slot * 2 + h) * NG + j])

    def b_at(slot, k):
        return bbuf.at[pl.ds(slot * PART + k * 32, 32), pl.ds(0, MAIN)]

    def t_at(slot, k):
        return tbuf.at[slot, pl.ds(k * 64, 64), :]

    def b_send(src_slot, k, dst_slot, device):
        send(b_at(src_slot, k), b_at(dst_slot, k), bsem.at[dst_slot * 2 + k], device)
        send(t_at(src_slot, k), t_at(dst_slot, k), tsem.at[dst_slot * 2 + k], device)

    def b_arrive(slot, k):
        arrive(b_at(slot, k), bsem.at[slot * 2 + k])
        arrive(t_at(slot, k), tsem.at[slot * 2 + k])

    def x_at(c, half=None):
        if half is None:
            return xbuf.at[c]
        return xbuf.at[c, pl.ds(half * (TOKENS // 2), TOKENS // 2), :]

    def x_send(c, half, sem, device, src=None):
        send(x_at(c, half) if src is None else src, x_at(c, half), xsem.at[sem], device)

    def x_arrive(c, half, sem):
        arrive(x_at(c, half), xsem.at[sem])

    to_right = [(h, j) for h in (0, 1) for j in range(NG)]
    to_left = [(h, j) for h in (1, 0) for j in range(NG)]
    to_pair = [(h, j) for j in range(NG) for h in (0, 1)]

    def own_pieces(first, last):
        for i in range(first, last):
            w_send(0, *to_right[i], 3, right)
            w_send(0, *to_left[i], 1, left)

    def own_to_pair(first, last):
        for i in range(first, last):
            w_send(0, *to_pair[i], 4, pair)

    x_send(col, None, 0, up, acts)
    x_send(col, None, 1, down, acts)
    own_pieces(0, 2)
    own_to_pair(0, 1)
    x_send(col, None, 9, twin, acts)

    own_ranks.wait()
    own_out.wait()
    raw = jnp.concatenate([out_raw[m].astype(F32) for m in range(MEMBERS)], axis=0)
    out_noise[...] = raw.astype(BF16)
    fit = jnp.concatenate(
        [
            jnp.full((4, 1), ranks[m].astype(F32), F32) / (MEMBERS * POP - 1) - 0.5
            for m in range(MEMBERS)
        ],
        axis=0,
    )
    scaled = raw * fit
    bbuf[pl.ds(0, PART), :] = scaled.astype(BF16)
    own_weight.wait()
    last = wbuf[0, :, pl.ds(MAIN, REST)].astype(F32)
    tbuf[0, pl.ds(0, 112), :] = jnp.concatenate(
        [last[g * 112 : g * 112 + 112] for g in range(4)], axis=1
    ).astype(BF16)
    tbuf[0, pl.ds(112, 16), :] = jnp.concatenate(
        [scaled[g * 16 : g * 16 + 16, MAIN:WIDE] for g in range(4)], axis=1
    ).astype(BF16)
    own_noise.wait()
    wide = jnp.concatenate([noise_raw[m].astype(F32) for m in range(MEMBERS)], axis=0)
    for c in range(COL):
        noise[c] = wide[:, c * FEAT : (c + 1) * FEAT].astype(BF16)

    for k, device, slot in ((0, right, 3), (1, left, 1), (0, pair, 4), (1, right, 3), (0, left, 1), (1, pair, 4)):
        b_send(0, k, slot, device)

    def a_at(slot):
        return abuf.at[:, pl.ds(slot * PART, PART), :]

    target = (ylo + mine // NX) % 2 * NX + (x + NX - mine % NX) % NX
    fetch = pltpu.make_async_remote_copy(
        src_ref=noise.at[pl.ds(2 * target, 2)],
        dst_ref=a_at(mine),
        send_sem=lsem.at[4],
        recv_sem=asem.at[0],
        device_id=(target, col),
        device_id_type=MESH,
    )
    keep = pltpu.make_async_copy(noise.at[pl.ds(2 * pop, 2)], a_at(0), lsem.at[5])

    @pl.when(mine > 0)
    def _():
        fetch.start()

    @pl.when(mine == 0)
    def _():
        keep.start()

    x_send(col, None, 2, far, acts)
    own_pieces(2, 4)

    c_down, c_up = col_at(3, 0, 0), col_at(1, 0, 0)
    c_far, c_opp = col_at(0, 1, 0), col_at(2, 0, 0)
    f_down, f_up, f_opp = col_at(3, 1, 0), col_at(1, 1, 0), col_at(2, 1, 0)

    def add_low(c):
        low[...] += lax.dot_general(
            xbuf[c],
            noise[c],
            (((1,), (1,)), ((), ())),
            preferred_element_type=F32,
        )

    def half(slot, h, k):
        return wbuf.at[slot, pl.ds(h * FEAT + k * 112, 112), pl.ds(*GROUPS[-1])]

    def relay(first, last):
        for j in range(first, last):
            w_arrive(3, 0, j)
            w_send(3, 0, j, 2, right)
            w_arrive(1, 1, j)
            w_send(1, 1, j, 2, left)

    def across(first, last):
        for j in range(first, last):
            for h in range(2):
                w_arrive(2, h, j)
                w_send(2, h, j, 6, pair)

    def pass_on(first, last):
        for i in range(first, last):
            h, j = to_pair[i]
            w_arrive(4, h, j)
            if j < NG - 1 or h == 0:
                w_send(4, h, j, 7, right)
            else:
                send(half(4, 1, 0), half(7, 1, 0), esem.at[1], right)
            if j < NG - 1 or h == 1:
                w_send(4, h, j, 5, left)
            else:
                send(half(4, 0, 0), half(5, 0, 0), esem.at[0], left)

    b_arrive(3, 0)
    b_send(3, 0, 2, right)
    b_arrive(1, 1)
    b_send(1, 1, 2, left)
    for k in range(2):
        b_arrive(4, k)
        b_send(4, k, 7, right)
        b_send(4, k, 5, left)
    own_pieces(4, 7)

    low[...] = jnp.zeros_like(low)
    own_acts.wait()
    add_low(col)

    x_arrive(c_down, None, 0)
    x_send(c_down, 0, 5, up)
    x_send(c_down, None, 10, twin)
    x_arrive(c_up, None, 1)
    x_send(c_up, 1, 6, down)
    x_send(c_up, None, 11, twin)

    @pl.when(mine > 0)
    def _():
        fetch.wait()

    @pl.when(mine == 0)
    def _():
        keep.wait()

    for dz, device in ((1, up), (3, down), (2, (pop, col_at(2, 0, 0)))):
        send(a_at(mine), a_at(mine), asem.at[2 * dz], device)
    send(a_at(mine), a_at(mine), asem.at[1], twin)

    for k in range(2):
        b_arrive(2, k)
        b_send(2, k, 6, pair)
    own_to_pair(1, 5)
    add_low(c_down)
    add_low(c_up)
    x_arrive(c_far, None, 2)
    x_send(c_far, None, 3, up)
    x_send(c_far, None, 4, down)
    x_send(c_far, None, 12, twin)
    own_pieces(7, 9)
    add_low(c_far)

    b_arrive(3, 1)
    b_arrive(1, 0)
    for slot in (7, 5, 6):
        for k in range(2):
            b_arrive(slot, k)
    def owner(dz, dc):
        return ((z + NZ - dz) % NZ) * 2 + (core * (1 - 2 * dc) + dc)

    for dz in (1, 3, 2):
        block = a_at(owner(dz, 0))
        arrive(block, asem.at[2 * dz])
        send(block, block, asem.at[2 * dz + 1], twin)
    for dz in range(NZ):
        arrive(a_at(owner(dz, 1)), asem.at[2 * dz + 1])

    @pl.loop(1, POP)
    def _(slot):
        packed = tbuf[slot].astype(F32)
        for g in range(4):
            mid = packed[:, g * REST : (g + 1) * REST].astype(BF16)
            wbuf[slot, pl.ds(g * 112, 112), pl.ds(MAIN, REST)] = mid[:112]
            bbuf[
                pl.ds(pl.multiple_of(slot * PART + g * 16, 16), 16), pl.ds(MAIN, REST)
            ] = mid[112:]

    squares = jnp.zeros((), F32)
    for h in range(2):
        block = lax.dot_general(
            abuf[h], bbuf[...], (((0,), (0,)), ((), ())), preferred_element_type=F32
        )
        delta[pl.ds(h * FEAT, FEAT), :] = block
        squares += jnp.sum(block * block)
    part[0] = jnp.full((1, 128), squares, F32)

    for i, device in pop_peers:
        send(part.at[0], parts.at[8 + i], rsem.at[8 + i], device)
    own_pieces(9, 10)
    own_to_pair(5, 8)
    relay(0, NG)
    x_arrive(c_opp, 0, 5)
    x_send(c_opp, 0, 15, twin)
    x_arrive(c_opp, 1, 6)
    x_send(c_opp, 1, 16, twin)
    add_low(c_opp)
    x_arrive(f_down, None, 3)
    x_send(f_down, 0, 7, up)
    x_send(f_down, None, 13, twin)
    x_arrive(f_up, None, 4)
    x_send(f_up, 1, 8, down)
    x_send(f_up, None, 14, twin)
    total = part[0]
    for i, _ in pop_peers:
        arrive(parts.at[8 + i], rsem.at[8 + i])
        total = total + parts[8 + i]
    part[1] = total
    add_low(f_down)
    add_low(f_up)
    send(part.at[1], parts.at[8], rsem.at[8], far)
    own_to_pair(8, 10)
    across(0, 1)
    pass_on(0, 4)

    def add_twin(dz, dy, *sems):
        c = col_at(dz, dy, 1)
        for i, sem in enumerate(sems):
            x_arrive(c, i if len(sems) > 1 else None, sem)
        add_low(c)

    add_twin(0, 0, 9)
    add_twin(3, 0, 10)
    across(1, 2)
    add_twin(1, 0, 11)
    add_twin(0, 1, 12)
    arrive(parts.at[8], rsem.at[8])
    part[2] = part[1] + parts[8]
    add_twin(2, 0, 15, 16)
    across(2, 3)
    for i, device in col_peers:
        send(part.at[2], parts.at[i], rsem.at[i], device)
    x_arrive(f_opp, 0, 7)
    x_send(f_opp, 0, 17, twin)
    x_arrive(f_opp, 1, 8)
    x_send(f_opp, 1, 18, twin)
    add_low(f_opp)
    add_twin(3, 1, 13)
    add_twin(1, 1, 14)
    across(3, 4)
    add_twin(2, 1, 17, 18)
    pass_on(4, 5)
    across(4, NG)

    rank = lax.broadcasted_iota(jnp.int32, (TOKENS, PART), 1) // 4
    token = lax.broadcasted_iota(jnp.int32, (TOKENS, PART), 0) // 64
    low[...] = jnp.where(rank == token, low[...] * 0.5, 0.0)

    def rows(i):
        return pl.ds(pl.multiple_of(i * TILE, TILE), TILE)

    @pl.loop(0, TOKENS // TILE)
    def _(i):
        left_over = low[rows(i), :]
        value = None
        for _ in range(3):
            term = left_over.astype(BF16)
            left_over = left_over - term.astype(F32)
            product = jnp.dot(term, out_noise[...], preferred_element_type=F32)
            value = product if value is None else value + product
        acc[rows(i), :] = value

    pass_on(5, 6)

    def dot(i, slot, h, cols):
        c = 2 * pop_at(slot // NX, slot % NX) + h
        return jnp.dot(
            xbuf[c, rows(i), :],
            wbuf[slot, pl.ds(h * FEAT, FEAT), cols],
            preferred_element_type=F32,
        )

    everything = pl.ds(0, WIDE)

    def blocks(slot):
        @pl.loop(0, TOKENS // TILE)
        def _(i):
            for h in range(2):
                acc[rows(i), :] += dot(i, slot, h, everything)

    blocks(0)
    pass_on(6, 7)
    for j in range(NG):
        w_arrive(3, 1, j)
        w_arrive(1, 0, j)
    send(half(1, 0, 1), half(5, 0, 1), esem.at[2], pair)
    send(half(3, 1, 1), half(7, 1, 1), esem.at[3], pair)
    blocks(1)
    pass_on(7, 9)
    blocks(3)
    pass_on(9, 10)
    blocks(4)
    blocks(2)

    total = part[2]
    for i, _ in col_peers:
        arrive(parts.at[i], rsem.at[i])
        total = total + parts[i]
    scale = lax.rsqrt(total / (D * F) + 1e-06)[0:1, 0:1]
    step = delta[...] * scale
    step_out[...] = step
    new_out[...] = (wbuf[0].astype(F32) + 0.01 * step).astype(BF16)
    for j in range(NG):
        for h in range(2):
            for slot in (5, 7, 6):
                if j < NG - 1 or (slot, h) not in ((5, 0), (7, 1)):
                    w_arrive(slot, h, j)
        if j == NG - 1:
            for i, (slot, h, k) in enumerate(((5, 0, 0), (7, 1, 0), (5, 0, 1), (7, 1, 1))):
                arrive(half(slot, h, k), esem.at[i])
            break
        cols = pl.ds(*GROUPS[j])

        @pl.loop(0, TOKENS // TILE)
        def _(i):
            value = acc[rows(i), cols]
            for slot in (5, 7, 6):
                for h in range(2):
                    value = value + dot(i, slot, h, cols)
            out[rows(i), cols] = value.astype(BF16)


    for copy in sent:
        copy.wait_send()


def put_out(
    out_v, step_v, new_v, wbuf, xbuf, acc, out, step_out, new_out, last, sem
):
    first = GROUPS[-1][0]
    cols = pl.ds(first, WIDE - first)
    ready = pl.ds(0, first)
    pairs = (
        (step_v, step_out),
        (out_v.at[:, ready], out.at[:, ready]),
        (new_v, new_out),
        (last, out.at[:, cols]),
    )
    writes = [
        pltpu.make_async_copy(src, dst, sem.at[i]) for i, (src, dst) in enumerate(pairs)
    ]
    for copy in writes[:3]:
        copy.start()
    pop = lax.axis_index("pop")
    x, ylo = pop % NX, pop // NX

    @pl.loop(0, TOKENS // TILE)
    def _(i):
        rows = pl.ds(pl.multiple_of(i * TILE, TILE), TILE)
        value = acc[rows, cols]
        for slot in (5, 7, 6):
            source = (1 - ylo) * NX + (x + slot % NX) % NX
            for h in range(2):
                value = value + jnp.dot(
                    xbuf[2 * source + h, rows, :],
                    wbuf[slot, pl.ds(h * FEAT, FEAT), cols],
                    preferred_element_type=F32,
                )
        last[rows, :] = value.astype(BF16)

    writes[3].start()
    for copy in writes:
        copy.wait()


def body(acts, weight, input_noise_factor, output_noise_factor, ranks):
    hbm = pl.BlockSpec(memory_space=pltpu.HBM)
    vmem = pl.BlockSpec(memory_space=pltpu.VMEM)
    made = pl.pallas_call(
        kernel,
        out_shape=(
            pltpu.VMEM((TOKENS, WIDE), BF16),
            pltpu.VMEM((ROWS, WIDE), F32),
            pltpu.VMEM((ROWS, WIDE), BF16),
            pltpu.VMEM((POP, ROWS, WIDE), BF16),
            pltpu.VMEM((COL, TOKENS, FEAT), BF16),
            pltpu.VMEM((TOKENS, WIDE), F32),
        ),
        in_specs=[hbm] * 5,
        out_specs=(vmem,) * 6,
        scratch_shapes=[
            pltpu.VMEM((2, POP * PART, FEAT), BF16),
            pltpu.VMEM((POP * PART, WIDE), BF16),
            pltpu.VMEM((POP, 128, 128), BF16),
            pltpu.SMEM((MEMBERS,), jnp.int32),
            pltpu.VMEM((MEMBERS, 4, D), BF16),
            pltpu.VMEM((MEMBERS, 4, WIDE), BF16),
            pltpu.VMEM((COL, PART, FEAT), BF16),
            pltpu.VMEM((PART, WIDE), BF16),
            pltpu.VMEM((TOKENS, PART), F32),
            pltpu.VMEM((ROWS, WIDE), F32),
            pltpu.VMEM((3, 1, 128), F32),
            pltpu.VMEM((16, 1, 128), F32),
            pltpu.SemaphoreType.DMA((POP * 2 * NG,)),
            pltpu.SemaphoreType.DMA((POP * 2,)),
            pltpu.SemaphoreType.DMA((POP * 2,)),
            pltpu.SemaphoreType.DMA((8,)),
            pltpu.SemaphoreType.DMA((4,)),
            pltpu.SemaphoreType.DMA((19,)),
            pltpu.SemaphoreType.DMA((16,)),
            pltpu.SemaphoreType.DMA((192,)),
            pltpu.SemaphoreType.DMA((13,)),
        ],
        compiler_params=pltpu.CompilerParams(
            collective_id=0, has_side_effects=True, vmem_limit_bytes=34 * 1024 * 1024
        ),
    )(
        acts.reshape(TOKENS, FEAT),
        weight,
        input_noise_factor,
        output_noise_factor,
        pltpu.with_memory_space_constraint(ranks, pltpu.HBM),
    )
    out, step_dir, new_weight = pl.pallas_call(
        put_out,
        out_shape=(
            jax.ShapeDtypeStruct((TOKENS, WIDE), BF16),
            jax.ShapeDtypeStruct((ROWS, WIDE), F32),
            jax.ShapeDtypeStruct((ROWS, WIDE), BF16),
        ),
        in_specs=[vmem] * 6,
        out_specs=(hbm,) * 3,
        scratch_shapes=[
            pltpu.VMEM((TOKENS, WIDE - GROUPS[-1][0]), BF16),
            pltpu.SemaphoreType.DMA((4,)),
        ],
        compiler_params=pltpu.CompilerParams(vmem_limit_bytes=4 * 1024 * 1024),
    )(*made)
    return (out.reshape(MEMBERS, TOKENS // MEMBERS, WIDE), step_dir, new_weight)


def solution(mesh):
    in_specs = (
        P("pop", None, "col"),
        P("pop", "col"),
        P("pop", None, None),
        P("pop", None, "col"),
        P("pop"),
    )
    out_specs = (P("pop", None, "col"), P("pop", "col"), P("pop", "col"))
    return jax.shard_map(body, mesh=mesh, in_specs=in_specs, out_specs=out_specs, check_vma=False)
```

```python
import jax
import jax.numpy as jnp
from jax import lax
from jax.experimental import pallas as pl
from jax.experimental.pallas import tpu as pltpu
from jax.sharding import PartitionSpec as P

D = 3584
F = 18944
NX = 4
NZ = 4
POP = 8
COL = 16
MEMBERS = 16
ROWS = 448
WIDE = 1184
MAIN = 1152
REST = WIDE - MAIN
FEAT = 224
TOKENS = 1024
PART = 64
GROUPS = ((0, 256), (256, 256), (512, 256), (768, 256), (1024, 128))
NG = len(GROUPS)
TILE = 256
MESH = pl.DeviceIdType.MESH
BF16 = jnp.bfloat16
F32 = jnp.float32


def kernel(
    acts,
    weight,
    noise_in,
    out_in,
    ranks_in,
    out,
    step_out,
    new_out,
    wbuf,
    xbuf,
    acc,
    abuf,
    bbuf,
    tbuf,
    ranks,
    noise_raw,
    out_raw,
    noise,
    out_noise,
    low,
    delta,
    part,
    parts,
    wsem,
    bsem,
    tsem,
    asem,
    esem,
    xsem,
    rsem,
    ssem,
    lsem,
):
    pop, col = lax.axis_index("pop"), lax.axis_index("col")
    x, ylo = pop % NX, pop // NX
    z, yhi, core = col // 4, (col // 2) % 2, col % 2
    mine = z * 2 + core

    def pop_at(dy, dx):
        return (ylo * (1 - 2 * dy) + dy) * NX + (x + dx) % NX

    def col_at(dz, dy, dc):
        return (
            ((z + dz) % NZ) * 4
            + (yhi * (1 - 2 * dy) + dy) * 2
            + (core * (1 - 2 * dc) + dc)
        )

    right, left = (pop_at(0, 1), col), (pop_at(0, 3), col)
    pair = (pop_at(1, 0), col)
    up, down = (pop, col_at(1, 0, 0)), (pop, col_at(3, 0, 0))
    far, twin = (pop, col_at(0, 1, 0)), (pop, col_at(0, 0, 1))
    pop_peers = [
        (dy * NX + dx, (pop_at(dy, dx), col))
        for dy in range(2)
        for dx in range(NX)
        if dy + dx > 0
    ]
    col_peers = [
        (dz * 2 + dc, (pop, col_at(dz, 0, dc)))
        for dz in range(NZ)
        for dc in range(2)
        if dz + dc > 0
    ]

    sent = []

    def send(src, dst, sem, device):
        copy = pltpu.make_async_remote_copy(
            src_ref=src,
            dst_ref=dst,
            send_sem=ssem.at[len(sent)],
            recv_sem=sem,
            device_id=device,
            device_id_type=MESH,
        )
        copy.start()
        sent.append(copy)

    def arrive(dst, sem):
        pltpu.make_async_remote_copy(
            src_ref=dst,
            dst_ref=dst,
            send_sem=ssem.at[0],
            recv_sem=sem,
            device_id=right,
            device_id_type=MESH,
        ).wait_recv()

    barrier = pltpu.get_barrier_semaphore()
    peers = [device for _, device in pop_peers + col_peers] + [far]
    for device in peers:
        pl.semaphore_signal(barrier, inc=1, device_id=device, device_id_type=MESH)
    own_noise = pltpu.make_async_copy(noise_in, noise_raw, lsem.at[0])
    own_out = pltpu.make_async_copy(out_in, out_raw, lsem.at[1])
    own_weight = pltpu.make_async_copy(weight, wbuf.at[0], lsem.at[2])
    own_acts = pltpu.make_async_copy(acts, xbuf.at[col], lsem.at[3])
    own_ranks = pltpu.make_async_copy(ranks_in, ranks, lsem.at[6])
    for copy in (own_ranks, own_out, own_noise, own_weight, own_acts):
        copy.start()

    pl.semaphore_wait(barrier, len(peers))

    def piece(h, j):
        return pl.ds(h * FEAT, FEAT), pl.ds(*GROUPS[j])

    def w_at(slot, h, j):
        r, c = piece(h, j)
        return wbuf.at[slot, r, c]

    def w_send(src_slot, h, j, dst_slot, device):
        r, c = piece(h, j)
        src = weight.at[r, c] if src_slot == 0 else wbuf.at[src_slot, r, c]
        send(src, w_at(dst_slot, h, j), wsem.at[(dst_slot * 2 + h) * NG + j], device)

    def w_arrive(slot, h, j):
        arrive(w_at(slot, h, j), wsem.at[(slot * 2 + h) * NG + j])

    def b_at(slot, k):
        return bbuf.at[pl.ds(slot * PART + k * 32, 32), pl.ds(0, MAIN)]

    def t_at(slot, k):
        return tbuf.at[slot, pl.ds(k * 64, 64), :]

    def b_send(src_slot, k, dst_slot, device):
        send(b_at(src_slot, k), b_at(dst_slot, k), bsem.at[dst_slot * 2 + k], device)
        send(t_at(src_slot, k), t_at(dst_slot, k), tsem.at[dst_slot * 2 + k], device)

    def b_arrive(slot, k):
        arrive(b_at(slot, k), bsem.at[slot * 2 + k])
        arrive(t_at(slot, k), tsem.at[slot * 2 + k])

    def x_at(c, half=None):
        if half is None:
            return xbuf.at[c]
        return xbuf.at[c, pl.ds(half * (TOKENS // 2), TOKENS // 2), :]

    def x_send(c, half, sem, device, src=None):
        send(x_at(c, half) if src is None else src, x_at(c, half), xsem.at[sem], device)

    def x_arrive(c, half, sem):
        arrive(x_at(c, half), xsem.at[sem])

    to_right = [(h, j) for h in (0, 1) for j in range(NG)]
    to_left = [(h, j) for h in (1, 0) for j in range(NG)]
    to_pair = [(h, j) for j in range(NG) for h in (0, 1)]

    def own_pieces(first, last):
        for i in range(first, last):
            w_send(0, *to_right[i], 3, right)
            w_send(0, *to_left[i], 1, left)

    def own_to_pair(first, last):
        for i in range(first, last):
            w_send(0, *to_pair[i], 4, pair)

    x_send(col, None, 0, up, acts)
    x_send(col, None, 1, down, acts)
    own_pieces(0, 2)
    own_to_pair(0, 1)
    x_send(col, None, 9, twin, acts)

    own_ranks.wait()
    own_out.wait()
    raw = jnp.concatenate([out_raw[m].astype(F32) for m in range(MEMBERS)], axis=0)
    out_noise[...] = raw.astype(BF16)
    fit = jnp.concatenate(
        [
            jnp.full((4, 1), ranks[m].astype(F32), F32) / (MEMBERS * POP - 1) - 0.5
            for m in range(MEMBERS)
        ],
        axis=0,
    )
    scaled = raw * fit
    bbuf[pl.ds(0, PART), :] = scaled.astype(BF16)
    own_weight.wait()
    last = wbuf[0, :, pl.ds(MAIN, REST)].astype(F32)
    tbuf[0, pl.ds(0, 112), :] = jnp.concatenate(
        [last[g * 112 : g * 112 + 112] for g in range(4)], axis=1
    ).astype(BF16)
    tbuf[0, pl.ds(112, 16), :] = jnp.concatenate(
        [scaled[g * 16 : g * 16 + 16, MAIN:WIDE] for g in range(4)], axis=1
    ).astype(BF16)
    own_noise.wait()
    wide = jnp.concatenate([noise_raw[m].astype(F32) for m in range(MEMBERS)], axis=0)
    for c in range(COL):
        noise[c] = wide[:, c * FEAT : (c + 1) * FEAT].astype(BF16)

    for k, device, slot in ((0, right, 3), (1, left, 1), (0, pair, 4), (1, right, 3), (0, left, 1), (1, pair, 4)):
        b_send(0, k, slot, device)

    def a_at(slot):
        return abuf.at[:, pl.ds(slot * PART, PART), :]

    target = (ylo + mine // NX) % 2 * NX + (x + NX - mine % NX) % NX
    fetch = pltpu.make_async_remote_copy(
        src_ref=noise.at[pl.ds(2 * target, 2)],
        dst_ref=a_at(mine),
        send_sem=lsem.at[4],
        recv_sem=asem.at[0],
        device_id=(target, col),
        device_id_type=MESH,
    )
    keep = pltpu.make_async_copy(noise.at[pl.ds(2 * pop, 2)], a_at(0), lsem.at[5])

    @pl.when(mine > 0)
    def _():
        fetch.start()

    @pl.when(mine == 0)
    def _():
        keep.start()

    x_send(col, None, 2, far, acts)
    own_pieces(2, 4)

    c_down, c_up = col_at(3, 0, 0), col_at(1, 0, 0)
    c_far, c_opp = col_at(0, 1, 0), col_at(2, 0, 0)
    f_down, f_up, f_opp = col_at(3, 1, 0), col_at(1, 1, 0), col_at(2, 1, 0)

    def add_low(c):
        low[...] += lax.dot_general(
            xbuf[c],
            noise[c],
            (((1,), (1,)), ((), ())),
            preferred_element_type=F32,
        )

    def half(slot, h, k):
        return wbuf.at[slot, pl.ds(h * FEAT + k * 112, 112), pl.ds(*GROUPS[-1])]

    def relay(first, last):
        for j in range(first, last):
            w_arrive(3, 0, j)
            w_send(3, 0, j, 2, right)
            w_arrive(1, 1, j)
            w_send(1, 1, j, 2, left)

    def across(first, last):
        for j in range(first, last):
            for h in range(2):
                w_arrive(2, h, j)
                w_send(2, h, j, 6, pair)

    def pass_on(first, last):
        for i in range(first, last):
            h, j = to_pair[i]
            w_arrive(4, h, j)
            if j < NG - 1 or h == 0:
                w_send(4, h, j, 7, right)
            else:
                send(half(4, 1, 0), half(7, 1, 0), esem.at[1], right)
            if j < NG - 1 or h == 1:
                w_send(4, h, j, 5, left)
            else:
                send(half(4, 0, 0), half(5, 0, 0), esem.at[0], left)

    b_arrive(3, 0)
    b_send(3, 0, 2, right)
    b_arrive(1, 1)
    b_send(1, 1, 2, left)
    for k in range(2):
        b_arrive(4, k)
        b_send(4, k, 7, right)
        b_send(4, k, 5, left)
    own_pieces(4, 7)

    low[...] = jnp.zeros_like(low)
    own_acts.wait()
    add_low(col)

    x_arrive(c_down, None, 0)
    x_send(c_down, 0, 5, up)
    x_send(c_down, None, 10, twin)
    x_arrive(c_up, None, 1)
    x_send(c_up, 1, 6, down)
    x_send(c_up, None, 11, twin)

    @pl.when(mine > 0)
    def _():
        fetch.wait()

    @pl.when(mine == 0)
    def _():
        keep.wait()

    for dz, device in ((1, up), (3, down), (2, (pop, col_at(2, 0, 0)))):
        send(a_at(mine), a_at(mine), asem.at[2 * dz], device)
    send(a_at(mine), a_at(mine), asem.at[1], twin)

    for k in range(2):
        b_arrive(2, k)
        b_send(2, k, 6, pair)
    own_to_pair(1, 5)
    add_low(c_down)
    add_low(c_up)
    x_arrive(c_far, None, 2)
    x_send(c_far, None, 3, up)
    x_send(c_far, None, 4, down)
    x_send(c_far, None, 12, twin)
    own_pieces(7, 9)
    add_low(c_far)

    b_arrive(3, 1)
    b_arrive(1, 0)
    for slot in (7, 5, 6):
        for k in range(2):
            b_arrive(slot, k)
    def owner(dz, dc):
        return ((z + NZ - dz) % NZ) * 2 + (core * (1 - 2 * dc) + dc)

    for dz in (1, 3, 2):
        block = a_at(owner(dz, 0))
        arrive(block, asem.at[2 * dz])
        send(block, block, asem.at[2 * dz + 1], twin)
    for dz in range(NZ):
        arrive(a_at(owner(dz, 1)), asem.at[2 * dz + 1])

    @pl.loop(1, POP)
    def _(slot):
        packed = tbuf[slot].astype(F32)
        for g in range(4):
            mid = packed[:, g * REST : (g + 1) * REST].astype(BF16)
            wbuf[slot, pl.ds(g * 112, 112), pl.ds(MAIN, REST)] = mid[:112]
            bbuf[
                pl.ds(pl.multiple_of(slot * PART + g * 16, 16), 16), pl.ds(MAIN, REST)
            ] = mid[112:]

    squares = jnp.zeros((), F32)
    for h in range(2):
        block = lax.dot_general(
            abuf[h], bbuf[...], (((0,), (0,)), ((), ())), preferred_element_type=F32
        )
        delta[pl.ds(h * FEAT, FEAT), :] = block
        squares += jnp.sum(block * block)
    part[0] = jnp.full((1, 128), squares, F32)

    for i, device in pop_peers:
        send(part.at[0], parts.at[8 + i], rsem.at[8 + i], device)
    own_pieces(9, 10)
    own_to_pair(5, 8)
    relay(0, NG)
    x_arrive(c_opp, 0, 5)
    x_send(c_opp, 0, 15, twin)
    x_arrive(c_opp, 1, 6)
    x_send(c_opp, 1, 16, twin)
    add_low(c_opp)
    x_arrive(f_down, None, 3)
    x_send(f_down, 0, 7, up)
    x_send(f_down, None, 13, twin)
    x_arrive(f_up, None, 4)
    x_send(f_up, 1, 8, down)
    x_send(f_up, None, 14, twin)
    total = part[0]
    for i, _ in pop_peers:
        arrive(parts.at[8 + i], rsem.at[8 + i])
        total = total + parts[8 + i]
    part[1] = total
    add_low(f_down)
    add_low(f_up)
    send(part.at[1], parts.at[8], rsem.at[8], far)
    own_to_pair(8, 10)
    early = len(sent)
    across(0, 1)
    pass_on(0, 4)

    def add_twin(dz, dy, *sems):
        c = col_at(dz, dy, 1)
        for i, sem in enumerate(sems):
            x_arrive(c, i if len(sems) > 1 else None, sem)
        add_low(c)

    add_twin(0, 0, 9)
    add_twin(3, 0, 10)
    across(1, 2)
    add_twin(1, 0, 11)
    add_twin(0, 1, 12)
    arrive(parts.at[8], rsem.at[8])
    part[2] = part[1] + parts[8]
    add_twin(2, 0, 15, 16)
    across(2, 3)
    for i, device in col_peers:
        send(part.at[2], parts.at[i], rsem.at[i], device)
    x_arrive(f_opp, 0, 7)
    x_send(f_opp, 0, 17, twin)
    x_arrive(f_opp, 1, 8)
    x_send(f_opp, 1, 18, twin)
    add_low(f_opp)
    add_twin(3, 1, 13)
    add_twin(1, 1, 14)
    across(3, 4)
    add_twin(2, 1, 17, 18)
    pass_on(4, 5)
    across(4, NG)

    rank = lax.broadcasted_iota(jnp.int32, (TOKENS, PART), 1) // 4
    token = lax.broadcasted_iota(jnp.int32, (TOKENS, PART), 0) // 64
    low[...] = jnp.where(rank == token, low[...] * 0.5, 0.0)

    def rows(i):
        return pl.ds(pl.multiple_of(i * TILE, TILE), TILE)

    @pl.loop(0, TOKENS // TILE)
    def _(i):
        left_over = low[rows(i), :]
        value = None
        for _ in range(3):
            term = left_over.astype(BF16)
            left_over = left_over - term.astype(F32)
            product = jnp.dot(term, out_noise[...], preferred_element_type=F32)
            value = product if value is None else value + product
        acc[rows(i), :] = value

    pass_on(5, 6)

    def dot(i, slot, h, cols):
        c = 2 * pop_at(slot // NX, slot % NX) + h
        return jnp.dot(
            xbuf[c, rows(i), :],
            wbuf[slot, pl.ds(h * FEAT, FEAT), cols],
            preferred_element_type=F32,
        )

    everything = pl.ds(0, WIDE)

    def blocks(slot):
        @pl.loop(0, TOKENS // TILE)
        def _(i):
            for h in range(2):
                acc[rows(i), :] += dot(i, slot, h, everything)

    blocks(0)
    pass_on(6, 7)
    for j in range(NG):
        w_arrive(3, 1, j)
        w_arrive(1, 0, j)
    send(half(1, 0, 1), half(5, 0, 1), esem.at[2], pair)
    send(half(3, 1, 1), half(7, 1, 1), esem.at[3], pair)
    blocks(1)
    pass_on(7, 9)
    blocks(3)
    pass_on(9, 10)
    blocks(4)
    blocks(2)

    total = part[2]
    for i, _ in col_peers:
        arrive(parts.at[i], rsem.at[i])
        total = total + parts[i]
    scale = lax.rsqrt(total / (D * F) + 1e-06)[0:1, 0:1]
    step = delta[...] * scale
    step_out[...] = step
    new_out[...] = (wbuf[0].astype(F32) + 0.01 * step).astype(BF16)
    for copy in sent[:early]:
        copy.wait_send()

    for j in range(NG):
        for h in range(2):
            for slot in (5, 7, 6):
                if j < NG - 1 or (slot, h) not in ((5, 0), (7, 1)):
                    w_arrive(slot, h, j)
        if j == NG - 1:
            for i, (slot, h, k) in enumerate(((5, 0, 0), (7, 1, 0), (5, 0, 1), (7, 1, 1))):
                arrive(half(slot, h, k), esem.at[i])
            break
        cols = pl.ds(*GROUPS[j])

        @pl.loop(0, TOKENS // TILE)
        def _(i):
            value = acc[rows(i), cols]
            for slot in (5, 7, 6):
                for h in range(2):
                    value = value + dot(i, slot, h, cols)
            out[rows(i), cols] = value.astype(BF16)


    for copy in sent[early:]:
        copy.wait_send()


def put_out(
    out_v, step_v, new_v, wbuf, xbuf, acc, out, step_out, new_out, last, sem
):
    first = GROUPS[-1][0]
    cols = pl.ds(first, WIDE - first)
    ready = pl.ds(0, first)
    pairs = (
        (step_v, step_out),
        (out_v.at[:, ready], out.at[:, ready]),
        (new_v, new_out),
        (last, out.at[:, cols]),
    )
    writes = [
        pltpu.make_async_copy(src, dst, sem.at[i]) for i, (src, dst) in enumerate(pairs)
    ]
    for copy in writes[:3]:
        copy.start()
    pop = lax.axis_index("pop")
    x, ylo = pop % NX, pop // NX

    @pl.loop(0, TOKENS // TILE)
    def _(i):
        rows = pl.ds(pl.multiple_of(i * TILE, TILE), TILE)
        value = acc[rows, cols]
        for slot in (5, 7, 6):
            source = (1 - ylo) * NX + (x + slot % NX) % NX
            for h in range(2):
                value = value + jnp.dot(
                    xbuf[2 * source + h, rows, :],
                    wbuf[slot, pl.ds(h * FEAT, FEAT), cols],
                    preferred_element_type=F32,
                )
        last[rows, :] = value.astype(BF16)

    writes[3].start()
    for copy in writes:
        copy.wait()


def body(acts, weight, input_noise_factor, output_noise_factor, ranks):
    hbm = pl.BlockSpec(memory_space=pltpu.HBM)
    vmem = pl.BlockSpec(memory_space=pltpu.VMEM)
    made = pl.pallas_call(
        kernel,
        out_shape=(
            pltpu.VMEM((TOKENS, WIDE), BF16),
            pltpu.VMEM((ROWS, WIDE), F32),
            pltpu.VMEM((ROWS, WIDE), BF16),
            pltpu.VMEM((POP, ROWS, WIDE), BF16),
            pltpu.VMEM((COL, TOKENS, FEAT), BF16),
            pltpu.VMEM((TOKENS, WIDE), F32),
        ),
        in_specs=[hbm] * 5,
        out_specs=(vmem,) * 6,
        scratch_shapes=[
            pltpu.VMEM((2, POP * PART, FEAT), BF16),
            pltpu.VMEM((POP * PART, WIDE), BF16),
            pltpu.VMEM((POP, 128, 128), BF16),
            pltpu.SMEM((MEMBERS,), jnp.int32),
            pltpu.VMEM((MEMBERS, 4, D), BF16),
            pltpu.VMEM((MEMBERS, 4, WIDE), BF16),
            pltpu.VMEM((COL, PART, FEAT), BF16),
            pltpu.VMEM((PART, WIDE), BF16),
            pltpu.VMEM((TOKENS, PART), F32),
            pltpu.VMEM((ROWS, WIDE), F32),
            pltpu.VMEM((3, 1, 128), F32),
            pltpu.VMEM((16, 1, 128), F32),
            pltpu.SemaphoreType.DMA((POP * 2 * NG,)),
            pltpu.SemaphoreType.DMA((POP * 2,)),
            pltpu.SemaphoreType.DMA((POP * 2,)),
            pltpu.SemaphoreType.DMA((8,)),
            pltpu.SemaphoreType.DMA((4,)),
            pltpu.SemaphoreType.DMA((19,)),
            pltpu.SemaphoreType.DMA((16,)),
            pltpu.SemaphoreType.DMA((192,)),
            pltpu.SemaphoreType.DMA((13,)),
        ],
        compiler_params=pltpu.CompilerParams(
            collective_id=0, has_side_effects=True, vmem_limit_bytes=34 * 1024 * 1024
        ),
    )(
        acts.reshape(TOKENS, FEAT),
        weight,
        input_noise_factor,
        output_noise_factor,
        pltpu.with_memory_space_constraint(ranks, pltpu.HBM),
    )
    out, step_dir, new_weight = pl.pallas_call(
        put_out,
        out_shape=(
            jax.ShapeDtypeStruct((TOKENS, WIDE), BF16),
            jax.ShapeDtypeStruct((ROWS, WIDE), F32),
            jax.ShapeDtypeStruct((ROWS, WIDE), BF16),
        ),
        in_specs=[vmem] * 6,
        out_specs=(hbm,) * 3,
        scratch_shapes=[
            pltpu.VMEM((TOKENS, WIDE - GROUPS[-1][0]), BF16),
            pltpu.SemaphoreType.DMA((4,)),
        ],
        compiler_params=pltpu.CompilerParams(vmem_limit_bytes=4 * 1024 * 1024),
    )(*made)
    return (out.reshape(MEMBERS, TOKENS // MEMBERS, WIDE), step_dir, new_weight)


def solution(mesh):
    in_specs = (
        P("pop", None, "col"),
        P("pop", "col"),
        P("pop", None, None),
        P("pop", None, "col"),
        P("pop"),
    )
    out_specs = (P("pop", None, "col"), P("pop", "col"), P("pop", "col"))
    return jax.shard_map(body, mesh=mesh, in_specs=in_specs, out_specs=out_specs, check_vma=False)
```
